32 devices in a mesh: grp: 2 (over y), band: 4 (over z), sub: 2 (over x), kern: 2 (over core).
Axes of the slice: x: 2, y: 2, z: 4, core: 2. Of those that a mesh axis runs over, the one named last changes fastest.
Arguments:
- screens: bfloat16 [32, 2, 64, 64], P('band'), may hold values from -6 to 6
- visibilities: bfloat16 [1024, 2, 128], P(('grp', 'band', 'sub', 'kern')), parts along dimension 0, may hold values from -6 to 6
- vis_columns: int32 [1024, 128], P(('grp', 'band', 'sub', 'kern')), parts along dimension 0, may hold values from 0 to 63
- band_route: int32 [1024, 1], P(('grp', 'band', 'sub', 'kern')), parts along dimension 0, may hold values from 0 to 3; in each aligned block of 32 rows (0 to 31, 32 to 63, ...) at most 16 rows name the same one
- screen_choice: int32 [1024], P(('grp', 'band', 'sub', 'kern')), parts along dimension 0, may hold values from 0 to 31
- offsets: int32 [1024, 2], P(('grp', 'band', 'sub', 'kern')), parts along dimension 0, may hold values from 0 to 7
- row_cell: int32 [1024], P(('grp', 'band', 'sub', 'kern')), parts along dimension 0, may hold values from 0 to 192
- col_cell: int32 [1024], P(('grp', 'band', 'sub', 'kern')), parts along dimension 0, may hold values from 0 to 896
Outputs:
- grid: float32 [2, 2048, 1024], P(None, ('grp', 'band', 'sub', 'kern')), parts along dimension 1
The draws below stay inside these ranges and needn't reach their ends.
There are 2 independent parts, one for each index of `grp`. The reference program is written for one: setup_inputs(seed, part) draws one part's arguments, and reference() takes and returns one part's arrays. A program takes and returns all parts, laid end to end along the dimension named above; an argument that names none is the same for every part. Nothing has to cross between parts.
Inputs may be any that keep to these rules, and one draw needn't show every extreme that they name: `band_route`: among the blocks of one device no band is named more than 16 times, a bound that some block reaches.
All inputs are finite; a program needn't handle non-finite values.
Results may differ from the reference program's by a relative error of at most 0.0058.
Values may be sent and summed in bfloat16 or wider, within the bound.
No kernel may reach another device: no remote copies, remote signals or barrier semaphores. Data moves between devices by JAX's collectives and lax.ppermute only.
A program may use at most 64 MiB of HBM per device.

```python
import math
import jax
import jax.numpy as jnp
import numpy as np
from jax import lax

KS = 64
OVERS = 8
VB = 128
BR = 256
NCOL = 1024
NB_DEV = 32
NK = 32
CAP = 16
NBLK = 512
NROW = 1024
N_BAND = 4


def touch_ends(result, own_key, smallest, top_value):
    spot = [jax.random.randint(jax.random.fold_in(own_key, axis), (), 0, length) for axis, length in enumerate(result.shape)]
    longest = result.shape.index(max(result.shape))
    beside = spot[:longest] + [(spot[longest] + 1) % result.shape[longest]] + spot[longest + 1:]
    return result.at[tuple(spot)].set(smallest).at[tuple(beside)].set(top_value)


def steps_of(own_key, extent, shards, smallest, high):
    level = 1.0
    for axis_at, blocks in shards:
        heights = jax.random.uniform(jax.random.fold_in(jax.random.fold_in(own_key, 6), axis_at), (blocks,), jnp.float32, smallest / len(shards), high / len(shards))
        level = level * jnp.repeat(jnp.exp(heights), extent[axis_at] // blocks).reshape((-1,) + (1,) * (len(extent) - 1 - axis_at))
    return level


def assign_block(stream_key, own, number, rows, number_of, top, limit, lean):
    order = jax.random.permutation(stream_key, number_of)
    packed, ordinary = shares(number_of, rows * top, limit, lean, True), shares(number_of, rows * top, limit, lean, False)
    places = jnp.arange(number_of)

    def named(lengths, offset_by):
        used = int((lengths > 0).sum())
        fixed = max(1, used // 4)
        passed = fixed + (places - fixed + offset_by * (used - fixed)) % max(1, number_of - fixed)
        return jnp.zeros((number_of,), jnp.int32).at[order[jnp.where(places < fixed, places, passed)]].set(jnp.asarray(lengths, jnp.int32))

    lengths = jnp.where(number % 4 == 0, named(packed, number // 4), named(ordinary, number - number // 4 - 1))
    mixed = jax.random.permutation(jax.random.fold_in(own, 3), number_of)
    giver, taker = mixed[0:number_of // 2 * 2:2], mixed[1:number_of // 2 * 2:2]
    margin = jnp.minimum(lengths[giver] - 1, limit - lengths[taker]) // 2
    margin = jnp.where((giver == order[0]) | (taker == order[0]) | (lengths[taker] == 0), 0, jnp.maximum(margin, 0))
    passed = jax.random.randint(jax.random.fold_in(own, 4), (number_of // 2,), 0, 1 << 20) % (margin + 1)
    lengths = lengths.at[giver].add(-passed).at[taker].add(passed)
    labels = jnp.searchsorted(jnp.cumsum(lengths), jnp.arange(rows * top), side="right").astype(jnp.int32)
    table = labels.reshape(top, rows).T
    table = table[jax.random.permutation(jax.random.fold_in(own, 1), rows)]
    offset_by = jax.random.randint(jax.random.fold_in(own, 2), (rows, 1), 0, top)
    return jnp.take_along_axis(table, (jnp.arange(top)[None, :] + offset_by) % top, axis=1)


def shares(number_of, total, most, slope, full):
    loads = [(1 << 20) // math.isqrt(rank ** slope) + 1 for rank in range(1, number_of + 1)]
    largest = most if full else min(most, max(-(-total // number_of), total * loads[0] // sum(loads)))
    least = 1 if total - largest >= number_of - 1 else 0
    counts, spare = [largest] + [least] * (number_of - 1), total - largest - least * (number_of - 1)
    while spare > 0:
        candidates = [i for i in range(1, number_of) if counts[i] < largest] or [i for i in range(1, number_of) if counts[i] < most]
        pool, budget = sum([loads[i] for i in candidates]), spare
        for i in candidates:
            extra = min(most - counts[i], max(1, budget * loads[i] // pool), spare)
            counts[i] = counts[i] + extra
            spare = spare - extra
    return np.array(counts)


def bell_draw(key, shape, spread, bound, split=(), held_as=jnp.bfloat16):
    level = steps_of(key, shape, split, -0.22, 0.18) if split else 1.0
    values = jax.random.normal(key, shape, jnp.float32) * spread * level
    return jnp.minimum(jnp.maximum(values, -bound), bound).astype(held_as)


def setup_inputs(seed: int = 0, part: int = 0) -> dict:
    arg_keys = jax.random.split(jax.random.key(seed), 9)
    part_splits = jax.random.split(jax.random.fold_in(arg_keys[8], part), 9)
    screens = bell_draw(arg_keys[0], (NK, 2, KS, KS), 1.0, 6.0, ((0, 4),))
    visibilities = bell_draw(part_splits[1], (NBLK, 2, VB), 1.0, 6.0, ((0, 16),))
    vis_columns = touch_ends(jax.random.randint(part_splits[2], (NBLK, VB), 0, KS), jax.random.fold_in(part_splits[2], 1), 0, KS - 1).astype(jnp.int32)
    band_route_keys = jax.random.split(jax.random.fold_in(part_splits[3], 1), NBLK // NB_DEV)
    band_route_turns = jax.random.permutation(jax.random.fold_in(part_splits[3], 3), NBLK // NB_DEV)
    band_route = jax.vmap(lambda own, number: assign_block(jax.random.fold_in(part_splits[3], 2), own, number, NB_DEV, N_BAND, 1, CAP, 2))(band_route_keys, band_route_turns).reshape((NBLK, 1))
    screen_choice = touch_ends(jax.random.randint(part_splits[4], (NBLK,), 0, NK), jax.random.fold_in(part_splits[4], 1), 0, NK - 1).astype(jnp.int32)
    offsets = touch_ends(jax.random.randint(part_splits[5], (NBLK, 2), 0, OVERS), jax.random.fold_in(part_splits[5], 1), 0, OVERS - 1).astype(jnp.int32)
    row_cell = touch_ends(jax.random.randint(part_splits[6], (NBLK,), 0, BR - KS + 1), jax.random.fold_in(part_splits[6], 1), 0, BR - KS).astype(jnp.int32)
    col_cell = touch_ends(jax.random.randint(part_splits[7], (NBLK,), 0, NCOL - 2 * KS + 1), jax.random.fold_in(part_splits[7], 1), 0, NCOL - 2 * KS).astype(jnp.int32)
    return {"screens": screens, "visibilities": visibilities, "vis_columns": vis_columns, "band_route": band_route, "screen_choice": screen_choice, "offsets": offsets, "row_cell": row_cell, "col_cell": col_cell}


ref_group = 16


def settle(array_in):
    return lax.optimization_barrier(array_in.astype(jnp.bfloat16)).astype(jnp.float32)


def dft_tables(support):
    centred = jnp.arange(support, dtype=jnp.float32) - support // 2
    fractions = jnp.arange(OVERS, dtype=jnp.float32) / OVERS
    frequency = centred[None, :, None] + fractions[:, None, None]
    phases = -2.0 * math.pi * frequency * centred[None, None, :] / support
    return settle(jnp.stack([jnp.cos(phases), jnp.sin(phases)], axis=1) / support)


def complex_product(left_side, right_side, pattern):
    left_side = left_side.astype(jnp.float32)
    right_side = right_side.astype(jnp.float32)
    left_real, left_imag = left_side[:, 0], left_side[:, 1]
    right_real, right_imag = right_side[:, 0], right_side[:, 1]
    real_part = jnp.einsum(pattern, left_real, right_real) - jnp.einsum(pattern, left_imag, right_imag)
    imag_part = jnp.einsum(pattern, left_real, right_imag) + jnp.einsum(pattern, left_imag, right_real)
    return jnp.stack([real_part, imag_part], axis=1)


def build_kernels(tables, chosen, row_off, col_off):
    row_table = jnp.take(tables, row_off, axis=0)
    col_table = jnp.take(tables, col_off, axis=0)
    half_dft = settle(complex_product(row_table, chosen, "bum,bml->bul"))
    return settle(complex_product(half_dft, col_table, "bul,bvl->buv"))


def block_patches(kernels, values, columns):
    support = kernels.shape[-1]
    patch_width = 2 * support
    count = kernels.shape[0]
    onehot = (columns[:, :, None] == jnp.arange(support, dtype=jnp.int32)[None, None, :]).astype(jnp.float32)
    column_line = settle(jnp.einsum("bzv,bvc->bzc", values.astype(jnp.float32), onehot))
    padded = jnp.pad(column_line, ((0, 0), (0, 0), (0, patch_width + 1 - support)))
    toeplitz = jnp.tile(padded, (1, 1, support))[:, :, :support * patch_width]
    toeplitz = toeplitz.reshape(count, 2, support, patch_width)
    return complex_product(kernels, toeplitz, "bxj,bjy->bxy")


def add_patches(grid_band, patches, rows_at, cols_at):
    for index_slot in range(patches.shape[0]):
        corner = (jnp.int32(0), rows_at[index_slot], cols_at[index_slot])
        current = lax.dynamic_slice(grid_band, corner, patches.shape[1:])
        grid_band = lax.dynamic_update_slice(grid_band, current + patches[index_slot], corner)
    return grid_band


def reference(screens, visibilities, vis_columns, band_route, screen_choice, offsets, row_cell, col_cell):
    tables = dft_tables(KS)
    global_rows = (band_route[:, 0] * BR + row_cell).astype(jnp.int32)
    grid_full = jnp.zeros((2, NROW, NCOL), jnp.float32)

    def grid_turn(group_index, grid_full):
        first = (group_index * ref_group).astype(jnp.int32)

        def take_group(source):
            return lax.dynamic_slice_in_dim(source, first, ref_group, 0)

        group_offsets = take_group(offsets)
        chosen = jnp.take(screens, take_group(screen_choice), axis=0)
        kernels = build_kernels(tables, chosen, group_offsets[:, 0], group_offsets[:, 1])
        patches = block_patches(kernels, take_group(visibilities), take_group(vis_columns))
        return add_patches(grid_full, patches, take_group(global_rows), take_group(col_cell))

    return lax.fori_loop(0, NBLK // ref_group, grid_turn, grid_full)
```

```python
import functools
import math

import jax
import jax.numpy as jnp
import numpy as np
from jax import lax
from jax.experimental import pallas as pl
from jax.experimental.pallas import tpu as pltpu
from jax.sharding import PartitionSpec as P

OVERS = 8
BR = 256
NCOL = 1024
LANES = 128
FIELDS = 8
UNROLL = 4
DIRECT_MOST = 4

f32, bf16, i32 = jnp.float32, jnp.bfloat16, jnp.int32


def dft_tables(support):
    centred = np.arange(support, dtype=np.float32) - np.float32(support // 2)
    fractions = np.arange(OVERS, dtype=np.float32) / np.float32(OVERS)
    frequency = centred[None, :, None] + fractions[:, None, None]
    phases = np.float32(-2.0 * math.pi) * frequency * centred[None, None, :] / np.float32(support)
    scale = np.float32(support)
    return (
        (np.cos(phases) / scale).astype(jnp.bfloat16).astype(np.float32),
        (np.sin(phases) / scale).astype(jnp.bfloat16).astype(np.float32),
    )


def table_constants(support, rows):
    real, imag = dft_tables(support)
    padded = np.zeros((2, OVERS, support + 2 * rows, 2 * support), np.float32)
    padded[0, :, rows : rows + support] = np.concatenate([real, imag], axis=2)
    padded[1, :, rows : rows + support] = np.concatenate([imag, -real], axis=2)
    real_t, imag_t = real.transpose(0, 2, 1), imag.transpose(0, 2, 1)
    top = np.concatenate([real_t, -imag_t], axis=2)
    low = np.concatenate([-imag_t, -real_t], axis=2)
    columns = np.concatenate([top, low], axis=1).astype(jnp.bfloat16)
    return padded.reshape(2, -1, 2 * support), columns


def iota(shape, axis):
    return lax.broadcasted_iota(i32, shape, axis)


def nt_dot(left, right):
    return lax.dot_general(left, right, (((1,), (1,)), ((), ())), preferred_element_type=f32)


def nn_dot(left, right):
    return jnp.dot(left, right, preferred_element_type=f32)


def send_kernel(
    band_count, splits, capacity, direct,
    screens, values, columns, route, choice, offsets, row_cell, col_cell,
    *refs,
):
    outs, line_ref = refs[:-1], refs[-1]
    blocks, width = columns.shape
    support = screens.shape[-1]
    me = lax.axis_index("band")
    for block in range(blocks):
        hits = iota((support, width), 0) == columns[pl.ds(block, 1), :]
        line = nt_dot(values[block], hits.astype(f32).astype(bf16))
        line_ref[0, pl.ds(block, 1), :] = line[0:1]
        line_ref[1, pl.ds(block, 1), :] = line[1:2]
    at_row, at_lane = iota((support, LANES), 0), iota((support, LANES), 1)
    place_re = (at_lane == (LANES - at_row) % LANES).astype(f32).astype(bf16)
    place_im = (at_lane == support - at_row).astype(f32).astype(bf16)
    lines = nn_dot(line_ref[0].astype(bf16), place_re) + nn_dot(line_ref[1].astype(bf16), place_im)
    target = route[...]
    slots = band_count * capacity
    match = (iota((band_count, blocks), 0) == target).astype(f32)
    earlier = (iota((blocks, blocks), 0) < iota((blocks, blocks), 1)).astype(f32).astype(bf16)
    before = nn_dot(match.astype(bf16), earlier)
    rank = jnp.sum(before * match, axis=0, keepdims=True).astype(i32)
    slot = target * capacity + rank
    pick = (iota((slots, blocks), 0) == slot).astype(f32).astype(bf16)
    column = col_cell[...]
    fields = [
        choice[...], offsets[pl.ds(0, 1), :], offsets[pl.ds(1, 1), :], row_cell[...],
        column // LANES, column % LANES, jnp.ones_like(column), jnp.zeros_like(column),
    ]
    field_at = iota((FIELDS, blocks), 0)
    table = jnp.zeros((FIELDS, blocks), i32)
    for index, field in enumerate(fields):
        table = jnp.where(field_at == index, field, table)
    spread = (iota((FIELDS, LANES), 0) == iota((FIELDS, LANES), 1)).astype(f32).astype(bf16)
    meta = nt_dot(pick, table.astype(f32).astype(bf16)).astype(bf16)
    payload = jnp.concatenate(
        [nn_dot(pick, lines.astype(bf16)), nn_dot(meta, spread)], axis=1
    )
    slot_ref = outs[-1]
    slot_ref[...] = payload
    share = screens.shape[0] // splits
    first = lax.axis_index("kern") * share if splits > 1 else 0
    outs = outs[:-1] if direct else [outs[0].at[step] for step in range(band_count)]
    for step, out in enumerate(outs):
        dest = partner(me, step, band_count) if direct else step
        mine = slot_ref[pl.ds(dest * capacity, capacity), :]
        out[pl.ds(0, capacity), :] = mine[:, :LANES].astype(bf16)
        out[pl.ds(capacity, capacity), :] = mine[:, LANES:].astype(bf16)
    for index in range(share):
        both = jnp.concatenate(
            [screens[first + index, 0].astype(f32), screens[first + index, 1].astype(f32)], axis=1
        ).astype(bf16)
        for out in outs:
            out[pl.ds(2 * capacity + index * support, support), :] = both


def partner(me, step, count):
    if count & (count - 1) == 0:
        return me ^ step
    return lax.rem(me + step, count)


def grid_kernel(
    band_count, kern_count, splits, held, deep, per_band, rows, support, direct, parts_of, *refs
):
    pieces, screen_parts = refs[: parts_of[0]], refs[parts_of[0] : parts_of[1]]
    row_tables, column_tables, out = refs[parts_of[1] : parts_of[1] + 3]
    screen_ref, line_ref, meta_vmem, meta_smem, total, sem = refs[parts_of[1] + 3 :]
    share = per_band // splits
    slices = [(piece, at) for piece in pieces for at in range(piece.shape[0])]
    lines = jnp.concatenate([piece[at, :held, :] for piece, at in slices], axis=0)
    metas = jnp.concatenate([piece[at, held : 2 * held, :] for piece, at in slices], axis=0)
    count = lines.shape[0]
    spread = (iota((FIELDS, LANES), 0) == iota((FIELDS, LANES), 1)).astype(f32).astype(bf16)
    fields = nt_dot(spread, metas)
    kern = lax.axis_index("kern")
    low = ((lax.axis_index("sub") * kern_count + kern) * rows).astype(f32)
    row_at = fields[3:4]
    live = (fields[6:7] > 0.5) & (row_at < low + rows) & (row_at + support > low)
    live = live.astype(f32)
    upper = (iota((count, count), 0) < iota((count, count), 1)).astype(f32).astype(bf16)
    rank = nn_dot(jnp.broadcast_to(live, (FIELDS, count)).astype(bf16), upper)[0:1]
    start = (low + rows - row_at) * live
    field_at = iota((FIELDS, count), 0)
    packed = jnp.where(field_at == 3, start, fields) * live
    pick = (iota((count, count), 0).astype(f32) == rank).astype(f32) * live
    pick = pick.astype(bf16)
    line_ref[...] = nn_dot(pick, lines)
    chosen = nt_dot(packed.astype(bf16), pick)
    number = jnp.sum(live)
    screen = chosen[0:1].astype(i32)
    me = lax.axis_index("band")
    band_of = screen // per_band
    if not direct:
        step_of = band_of
    elif band_count & (band_count - 1) == 0:
        step_of = band_of ^ me
    else:
        step_of = (band_of - me + band_count) % band_count
    within = screen % per_band
    place = step_of * share + within % share
    if splits > 1:
        place = place + ((within // share) != kern).astype(i32) * (band_count * share)
    table_row = chosen[1:2].astype(i32) * (support + 2 * rows) + chosen[3:4].astype(i32)
    col = chosen[4:5].astype(i32) * LANES + chosen[5:6].astype(i32)
    slot_table = jnp.where(field_at == 0, place, 0)
    slot_table = jnp.where(field_at == 1, table_row, slot_table)
    slot_table = jnp.where(field_at == 2, chosen[2:3].astype(i32), slot_table)
    slot_table = jnp.where(field_at == 3, col, slot_table)
    slot_table = jnp.where(field_at == 4, number.astype(i32), slot_table)
    meta_vmem[...] = slot_table
    copy = pltpu.make_async_copy(meta_vmem, meta_smem, sem)
    copy.start()
    lane = iota((support, LANES), 1)
    sign = jnp.where(lane < support, -1.0, 1.0).astype(f32)
    for part_at, part in enumerate(screen_parts):
        for step in range(band_count):
            for index in range(share):
                base = deep + index * support
                both = part[step, pl.ds(base, support), :]
                turned = pltpu.roll(both.astype(f32), support, 1) * sign
                at = ((part_at * band_count + step) * share + index) * 2 * support
                screen_ref[pl.ds(at, support), :] = both
                screen_ref[pl.ds(at + support, support), :] = turned.astype(bf16)
    total[...] = jnp.zeros_like(total)
    copy.wait()
    y_at, l_at = iota((2 * support, LANES), 0), iota((2 * support, LANES), 1)
    lag = y_at - l_at % support
    keep = ((lag >= 0) & (lag < support)).astype(f32).astype(bf16)
    wide = 2 * support

    def turn(index, carry):
        ids = [index * UNROLL + extra for extra in range(UNROLL)]
        halves = []
        for k in ids:
            at = meta_smem[1, k]
            left = jnp.concatenate(
                [row_tables[0, pl.ds(at, rows), :], row_tables[1, pl.ds(at, rows), :]], axis=0
            ).astype(bf16)
            right = screen_ref[pl.ds(pl.multiple_of(meta_smem[0, k] * wide, wide), wide), :]
            halves.append(nn_dot(left, right).astype(bf16))
        kernels = [
            nn_dot(half, column_tables[meta_smem[2, k]]).astype(bf16)
            for half, k in zip(halves, ids)
        ]
        patches = []
        for kernel, k in zip(kernels, ids):
            line = jnp.broadcast_to(line_ref[pl.ds(k, 1), :], (wide, LANES))
            skewed = pltpu.roll(line, 0, 1, stride=1, stride_axis=0)
            patches.append(nt_dot(skewed.astype(bf16) * keep, kernel))
        for patch, k in zip(patches, ids):
            window = pl.ds(meta_smem[3, k], wide)
            total[window, :] = total[window, :] + patch
        return carry

    turns = (meta_smem[4, 0] + (UNROLL - 1)) // UNROLL
    lax.fori_loop(0, turns, turn, 0)
    for at in range(0, NCOL, LANES):
        turned = total[pl.ds(at, LANES), :].T
        out[0, :, pl.ds(at, LANES)] = turned[:rows]
        out[1, :, pl.ds(at, LANES)] = turned[rows:]


def exchange(parts, axis, count):
    if count & (count - 1) == 0:
        perms = [[(i, i ^ step) for i in range(count)] for step in range(count)]
    else:
        perms = [[((i + step) % count, i) for i in range(count)] for step in range(count)]
    return [parts[0]] + [
        lax.ppermute(parts[step], axis, perms[step]) for step in range(1, count)
    ]


def body(
    screens, visibilities, vis_columns, band_route, screen_choice, offsets, row_cell, col_cell
):
    band_count = lax.axis_size("band")
    sub_count, kern_count = lax.axis_size("sub"), lax.axis_size("kern")
    per_band, _, support, _ = screens.shape
    blocks = visibilities.shape[0]
    capacity = 2 * blocks // band_count
    rows = BR // (sub_count * kern_count)
    members = sub_count * kern_count
    group = ("sub", "kern")
    direct = band_count <= DIRECT_MOST and members in (1, 2, 4)
    splits = 2 if kern_count == 2 and per_band % 2 == 0 else 1
    share = per_band // splits
    depth = 2 * capacity + share * support
    vmem = pl.BlockSpec(memory_space=pltpu.VMEM)
    if direct:
        messages = [jax.ShapeDtypeStruct((depth, LANES), bf16)] * band_count
    else:
        messages = [jax.ShapeDtypeStruct((band_count, depth, LANES), bf16)]
    sent = pl.pallas_call(
        functools.partial(send_kernel, band_count, splits, capacity, direct),
        out_shape=messages + [jax.ShapeDtypeStruct((band_count * capacity, 2 * LANES), f32)],
        in_specs=[vmem] * 8,
        out_specs=[vmem] * (len(messages) + 1),
        scratch_shapes=[pltpu.VMEM((2, blocks, support), f32)],
    )(
        screens, visibilities, vis_columns, band_route.reshape(1, blocks),
        screen_choice.reshape(1, blocks), offsets.T, row_cell.reshape(1, blocks),
        col_cell.reshape(1, blocks),
    )
    count = members * band_count * capacity
    if direct:
        own = jnp.stack(exchange(sent[:-1], "band", band_count))
        slots = own[:, : 2 * capacity]
        pieces, screen_parts, held, deep = [own], [own], capacity, 2 * capacity
        for step in range(1, members):
            whole = splits > 1 and step == 1
            perm = [(i, i ^ step) for i in range(members)]
            got = lax.ppermute(own if whole else slots, group, perm)
            pieces.append(got)
            if whole:
                screen_parts.append(got)
    else:
        own = lax.all_to_all(sent[0], "band", 0, 0, tiled=True)
        slots = lax.all_gather(own[:, : 2 * capacity], group, axis=0, tiled=True)
        slots = slots.reshape(members * band_count, 2, capacity, LANES)
        pieces = [slots.transpose(1, 0, 2, 3).reshape(1, 2 * count, LANES)]
        screen_parts, held, deep = [own[:, 2 * capacity :]], count, 0
        if splits > 1:
            perm = [(i, i ^ 1) for i in range(kern_count)]
            screen_parts.append(lax.ppermute(screen_parts[0], "kern", perm))
    row_tables, column_tables = table_constants(support, rows)
    parts_of = (len(pieces), len(pieces) + len(screen_parts))
    return pl.pallas_call(
        functools.partial(
            grid_kernel, band_count, kern_count, splits, held, deep, per_band, rows, support,
            direct, parts_of,
        ),
        out_shape=jax.ShapeDtypeStruct((2, rows, NCOL), f32),
        in_specs=[vmem] * (parts_of[1] + 2),
        out_specs=vmem,
        scratch_shapes=[
            pltpu.VMEM((per_band * band_count * 2 * support, LANES), bf16),
            pltpu.VMEM((count, LANES), f32),
            pltpu.VMEM((FIELDS, count), i32),
            pltpu.SMEM((FIELDS, count), i32),
            pltpu.VMEM((NCOL, 2 * rows), f32),
            pltpu.SemaphoreType.DMA(()),
        ],
    )(*pieces, *screen_parts, jnp.asarray(row_tables), jnp.asarray(column_tables))


def solution(mesh):
    in_specs = (
        P("band", None, None, None),
        P(("grp", "band", "sub", "kern"), None, None),
        P(("grp", "band", "sub", "kern"), None),
        P(("grp", "band", "sub", "kern"), None),
        P(("grp", "band", "sub", "kern")),
        P(("grp", "band", "sub", "kern"), None),
        P(("grp", "band", "sub", "kern")),
        P(("grp", "band", "sub", "kern")),
    )
    out_specs = P(None, ("grp", "band", "sub", "kern"), None)
    return jax.shard_map(body, mesh=mesh, in_specs=in_specs, out_specs=out_specs, check_vma=False)
```

```python
import functools
import math

import jax
import jax.numpy as jnp
import numpy as np
from jax import lax
from jax.experimental import pallas as pl
from jax.experimental.pallas import tpu as pltpu
from jax.sharding import PartitionSpec as P

OVERS = 8
BR = 256
NCOL = 1024
LANES = 128
FIELDS = 8
UNROLL = 16
DIRECT_MOST = 4
VMEM_GRANT = 16 * 1024 * 1024

f32, bf16, i32 = jnp.float32, jnp.bfloat16, jnp.int32


def dft_tables(support):
    centred = np.arange(support, dtype=np.float32) - np.float32(support // 2)
    fractions = np.arange(OVERS, dtype=np.float32) / np.float32(OVERS)
    frequency = centred[None, :, None] + fractions[:, None, None]
    phases = np.float32(-2.0 * math.pi) * frequency * centred[None, None, :] / np.float32(support)
    scale = np.float32(support)
    return (
        (np.cos(phases) / scale).astype(jnp.bfloat16).astype(np.float32),
        (np.sin(phases) / scale).astype(jnp.bfloat16).astype(np.float32),
    )


def table_constants(support, rows):
    real, imag = dft_tables(support)
    padded = np.zeros((OVERS, support + 2 * rows, 2 * support), np.float32)
    padded[:, rows : rows + support] = np.concatenate([real, imag], axis=2)
    top = np.concatenate([real, -imag], axis=2)
    low = np.concatenate([imag, real], axis=2)
    columns = np.concatenate([top, low], axis=1).astype(jnp.bfloat16)
    return padded.reshape(-1, 2 * support), columns


def in_hbm(array):
    return pltpu.with_memory_space_constraint(array, pltpu.HBM)


def iota(shape, axis):
    return lax.broadcasted_iota(i32, shape, axis)


def nt_dot(left, right):
    return lax.dot_general(left, right, (((1,), (1,)), ((), ())), preferred_element_type=f32)


def nn_dot(left, right):
    return jnp.dot(left, right, preferred_element_type=f32)


def send_kernel(
    band_count, splits, capacity, direct,
    *refs,
):
    sources, outs, held = refs[:8], refs[8:-10], refs[-10:-2]
    line_ref, sems = refs[-2:]
    share, _, support, _ = held[0].shape
    first = lax.axis_index("kern") * share if splits > 1 else 0
    copies = []
    for index in (2, 1, 3, 4, 5, 6, 7, 0):
        source = sources[index].at[pl.ds(first, share)] if index == 0 else sources[index]
        copies.append(pltpu.make_async_copy(source, held[index], sems.at[index]))
    for copy in copies:
        copy.start()
    screens, values, columns, route, choice, offsets, row_cell, col_cell = held
    blocks, width = columns.shape
    me = lax.axis_index("band")
    for copy in copies:
        copy.wait()
    for block in range(blocks):
        hits = iota((support, width), 0) == columns[pl.ds(block, 1), :]
        line = nt_dot(values[block], hits.astype(f32).astype(bf16))
        line_ref[0, pl.ds(block, 1), :] = line[0:1]
        line_ref[1, pl.ds(block, 1), :] = line[1:2]
    at_row, at_lane = iota((support, LANES), 0), iota((support, LANES), 1)
    place_re = (at_lane == (LANES - at_row) % LANES).astype(f32).astype(bf16)
    place_im = (at_lane == support - at_row).astype(f32).astype(bf16)
    lines = nn_dot(line_ref[0].astype(bf16), place_re) + nn_dot(line_ref[1].astype(bf16), place_im)
    target = route[...]
    slots = band_count * capacity
    match = (iota((band_count, blocks), 0) == target).astype(f32)
    earlier = (iota((blocks, blocks), 0) < iota((blocks, blocks), 1)).astype(f32).astype(bf16)
    before = nn_dot(match.astype(bf16), earlier)
    rank = jnp.sum(before * match, axis=0, keepdims=True).astype(i32)
    slot = target * capacity + rank
    pick = (iota((slots, blocks), 0) == slot).astype(f32).astype(bf16)
    column = col_cell[...]
    fields = [
        choice[...], offsets[pl.ds(0, 1), :], offsets[pl.ds(1, 1), :], row_cell[...],
        column // LANES, column % LANES, jnp.ones_like(column), jnp.zeros_like(column),
    ]
    field_at = iota((FIELDS, blocks), 0)
    table = jnp.zeros((FIELDS, blocks), i32)
    for index, field in enumerate(fields):
        table = jnp.where(field_at == index, field, table)
    spread = (iota((FIELDS, LANES), 0) == iota((FIELDS, LANES), 1)).astype(f32).astype(bf16)
    meta = nt_dot(pick, table.astype(f32).astype(bf16)).astype(bf16)
    payload = jnp.concatenate(
        [nn_dot(pick, lines.astype(bf16)), nn_dot(meta, spread)], axis=1
    )
    slot_ref = outs[-1]
    slot_ref[...] = payload
    outs = outs[:-1] if direct else [outs[0].at[step] for step in range(band_count)]
    for step, out in enumerate(outs):
        dest = partner(me, step, band_count) if direct else step
        mine = slot_ref[pl.ds(dest * capacity, capacity), :]
        out[pl.ds(0, capacity), :] = mine[:, :LANES].astype(bf16)
        out[pl.ds(capacity, capacity), :] = mine[:, LANES:].astype(bf16)
    for index in range(share):
        both = jnp.concatenate(
            [screens[index, 0].astype(f32), screens[index, 1].astype(f32)], axis=1
        ).astype(bf16)
        for out in outs:
            out[pl.ds(2 * capacity + index * support, support), :] = both


def partner(me, step, count):
    if count & (count - 1) == 0:
        return me ^ step
    return lax.rem(me + step, count)


def grid_kernel(
    band_count, kern_count, splits, held, deep, per_band, rows, support, direct, parts_of, *refs
):
    pieces, screen_parts = refs[: parts_of[0]], refs[parts_of[0] : parts_of[1]]
    row_tables, column_tables, out = refs[parts_of[1] : parts_of[1] + 3]
    screen_ref, line_ref, meta_vmem, meta_smem, total, half_ref, kernel_ref, skew_ref, stage, sem, sems = (
        refs[parts_of[1] + 3 :]
    )
    share = per_band // splits
    slices = [(piece, at) for piece in pieces for at in range(piece.shape[0])]
    lines = jnp.concatenate([piece[at, :held, :] for piece, at in slices], axis=0)
    metas = jnp.concatenate([piece[at, held : 2 * held, :] for piece, at in slices], axis=0)
    count = lines.shape[0]
    spread = (iota((FIELDS, LANES), 0) == iota((FIELDS, LANES), 1)).astype(f32).astype(bf16)
    fields = nt_dot(spread, metas)
    kern = lax.axis_index("kern")
    low = ((lax.axis_index("sub") * kern_count + kern) * rows).astype(f32)
    row_at = fields[3:4]
    live = (fields[6:7] > 0.5) & (row_at < low + rows) & (row_at + support > low)
    live = live.astype(f32)
    upper = (iota((count, count), 0) < iota((count, count), 1)).astype(f32).astype(bf16)
    rank = nn_dot(jnp.broadcast_to(live, (FIELDS, count)).astype(bf16), upper)[0:1]
    start = (low + rows - row_at) * live
    field_at = iota((FIELDS, count), 0)
    packed = jnp.where(field_at == 3, start, fields) * live
    pick = (iota((count, count), 0).astype(f32) == rank).astype(f32) * live
    pick = pick.astype(bf16)
    line_ref[...] = nn_dot(pick, lines)
    chosen = nt_dot(packed.astype(bf16), pick)
    number = jnp.sum(live)
    screen = chosen[0:1].astype(i32)
    me = lax.axis_index("band")
    band_of = screen // per_band
    if not direct:
        step_of = band_of
    elif band_count & (band_count - 1) == 0:
        step_of = band_of ^ me
    else:
        step_of = (band_of - me + band_count) % band_count
    within = screen % per_band
    place = step_of * share + within % share
    if splits > 1:
        place = place + ((within // share) != kern).astype(i32) * (band_count * share)
    table_row = chosen[1:2].astype(i32) * (support + 2 * rows) + chosen[3:4].astype(i32)
    col = chosen[4:5].astype(i32) * LANES + chosen[5:6].astype(i32)
    slot_table = jnp.where(field_at == 0, place, 0)
    slot_table = jnp.where(field_at == 1, table_row, slot_table)
    slot_table = jnp.where(field_at == 2, chosen[2:3].astype(i32), slot_table)
    slot_table = jnp.where(field_at == 3, col, slot_table)
    slot_table = jnp.where(field_at == 4, number.astype(i32), slot_table)
    meta_vmem[:, pl.ds(0, count)] = slot_table
    meta_vmem[:, pl.ds(count, LANES)] = jnp.zeros((FIELDS, LANES), i32)
    copy = pltpu.make_async_copy(meta_vmem, meta_smem, sem)
    copy.start()
    lane = iota((support, LANES), 1)
    sign = jnp.where(lane < support, -1.0, 1.0).astype(f32)
    for part_at, part in enumerate(screen_parts):
        for step in range(band_count):
            for index in range(share):
                base = deep + index * support
                both = part[step, pl.ds(base, support), :]
                turned = pltpu.roll(both.astype(f32), support, 1) * sign
                at = ((part_at * band_count + step) * share + index) * 2 * support
                screen_ref[pl.ds(at, support), :] = both
                screen_ref[pl.ds(at + support, support), :] = turned.astype(bf16)
    total[...] = jnp.zeros_like(total)
    y_at, l_at = iota((2 * support, LANES), 0), iota((2 * support, LANES), 1)
    lag = y_at - l_at % support
    keep = ((lag >= 0) & (lag < support)).astype(f32).astype(bf16)
    wide = 2 * support
    copy.wait()

    def turn(index, carry):
        ids = [index * UNROLL + extra for extra in range(UNROLL)]
        for at, k in enumerate(ids):
            left = row_tables[pl.ds(meta_smem[1, k], rows), :].astype(bf16)
            right = screen_ref[pl.ds(pl.multiple_of(meta_smem[0, k] * wide, wide), wide), :]
            half_ref[at] = nn_dot(left, right).astype(bf16)
        for at, k in enumerate(ids):
            line = jnp.broadcast_to(line_ref[pl.ds(k, 1), :], (wide, LANES))
            skew_ref[at] = pltpu.roll(line, 0, 1, stride=1, stride_axis=0).astype(bf16) * keep
        for at, k in enumerate(ids):
            both = nt_dot(column_tables[meta_smem[2, k]], half_ref[at]).astype(bf16)
            real, imag = both[:support], both[support:]
            kernel_ref[at, pl.ds(0, support), :] = jnp.concatenate([real, imag], axis=1)
            kernel_ref[at, pl.ds(support, support), :] = jnp.concatenate([-imag, real], axis=1)
        for at, k in enumerate(ids):
            window = pl.ds(meta_smem[3, k], wide)
            total[window, :] = total[window, :] + nn_dot(skew_ref[at], kernel_ref[at])
        return carry

    turns = (meta_smem[4, 0] + (UNROLL - 1)) // UNROLL
    lax.fori_loop(0, turns, turn, 0)
    writes = []
    for at in range(NCOL // LANES):
        turned = total[pl.ds(at * LANES, LANES), :].T
        stage[at, 0] = turned[:rows]
        stage[at, 1] = turned[rows:]
        target = out.at[:, :, pl.ds(at * LANES, LANES)]
        writes.append(pltpu.make_async_copy(stage.at[at], target, sems.at[at]))
        writes[-1].start()
    for write in writes:
        write.wait()


def table_kernel(row_source, column_source, row_tables, column_tables, sems):
    copies = [
        pltpu.make_async_copy(row_source, row_tables, sems.at[0]),
        pltpu.make_async_copy(column_source, column_tables, sems.at[1]),
    ]
    for copy in copies:
        copy.start()
    for copy in copies:
        copy.wait()


def exchange(parts, axis, count):
    if count & (count - 1) == 0:
        perms = [[(i, i ^ step) for i in range(count)] for step in range(count)]
    else:
        perms = [[((i + step) % count, i) for i in range(count)] for step in range(count)]
    return [parts[0]] + [
        lax.ppermute(parts[step], axis, perms[step]) for step in range(1, count)
    ]


def body(
    screens, visibilities, vis_columns, band_route, screen_choice, offsets, row_cell, col_cell
):
    band_count = lax.axis_size("band")
    sub_count, kern_count = lax.axis_size("sub"), lax.axis_size("kern")
    per_band, _, support, _ = screens.shape
    blocks = visibilities.shape[0]
    capacity = 2 * blocks // band_count
    rows = BR // (sub_count * kern_count)
    members = sub_count * kern_count
    group = ("sub", "kern")
    direct = band_count <= DIRECT_MOST and members in (1, 2, 4)
    splits = 2 if kern_count == 2 and per_band % 2 == 0 else 1
    share = per_band // splits
    depth = 2 * capacity + share * support
    vmem = pl.BlockSpec(memory_space=pltpu.VMEM)
    hbm = pl.BlockSpec(memory_space=pltpu.HBM)
    grant = pltpu.CompilerParams(vmem_limit_bytes=VMEM_GRANT)
    if direct:
        messages = [jax.ShapeDtypeStruct((depth, LANES), bf16)] * band_count
    else:
        messages = [jax.ShapeDtypeStruct((band_count, depth, LANES), bf16)]
    sent = pl.pallas_call(
        functools.partial(send_kernel, band_count, splits, capacity, direct),
        out_shape=messages + [jax.ShapeDtypeStruct((band_count * capacity, 2 * LANES), f32)],
        in_specs=[hbm] * 8,
        out_specs=[vmem] * (len(messages) + 1),
        scratch_shapes=[
            pltpu.VMEM((share,) + screens.shape[1:], bf16),
            pltpu.VMEM(visibilities.shape, bf16),
            pltpu.VMEM(vis_columns.shape, i32),
            pltpu.VMEM((1, blocks), i32),
            pltpu.VMEM((1, blocks), i32),
            pltpu.VMEM((2, blocks), i32),
            pltpu.VMEM((1, blocks), i32),
            pltpu.VMEM((1, blocks), i32),
            pltpu.VMEM((2, blocks, support), f32),
            pltpu.SemaphoreType.DMA((8,)),
        ],
        compiler_params=grant,
    )(
        *map(
            in_hbm,
            (
                screens, visibilities, vis_columns, band_route.reshape(1, blocks),
                screen_choice.reshape(1, blocks), offsets.T, row_cell.reshape(1, blocks),
                col_cell.reshape(1, blocks),
            ),
        )
    )
    count = members * band_count * capacity
    if direct:
        own = jnp.stack(exchange(sent[:-1], "band", band_count))
        slots = own[:, : 2 * capacity]
        pieces, screen_parts, held, deep = [own], [own], capacity, 2 * capacity
        for step in range(1, members):
            whole = splits > 1 and step == 1
            perm = [(i, i ^ step) for i in range(members)]
            got = lax.ppermute(own if whole else slots, group, perm)
            pieces.append(got)
            if whole:
                screen_parts.append(got)
    else:
        own = lax.all_to_all(sent[0], "band", 0, 0, tiled=True)
        slots = lax.all_gather(own[:, : 2 * capacity], group, axis=0, tiled=True)
        slots = slots.reshape(members * band_count, 2, capacity, LANES)
        pieces = [slots.transpose(1, 0, 2, 3).reshape(1, 2 * count, LANES)]
        screen_parts, held, deep = [own[:, 2 * capacity :]], count, 0
        if splits > 1:
            perm = [(i, i ^ 1) for i in range(kern_count)]
            screen_parts.append(lax.ppermute(screen_parts[0], "kern", perm))
    tables = [jnp.asarray(table) for table in table_constants(support, rows)]
    tables = pl.pallas_call(
        table_kernel,
        out_shape=[jax.ShapeDtypeStruct(table.shape, table.dtype) for table in tables],
        in_specs=[hbm] * 2,
        out_specs=[vmem] * 2,
        scratch_shapes=[pltpu.SemaphoreType.DMA((2,))],
        compiler_params=grant,
        cost_estimate=pl.CostEstimate(flops=0, bytes_accessed=1 << 21, transcendentals=0),
    )(*map(in_hbm, tables))
    parts_of = (len(pieces), len(pieces) + len(screen_parts))
    return pl.pallas_call(
        functools.partial(
            grid_kernel, band_count, kern_count, splits, held, deep, per_band, rows, support,
            direct, parts_of,
        ),
        out_shape=jax.ShapeDtypeStruct((2, rows, NCOL), f32),
        in_specs=[vmem] * (parts_of[1] + 2),
        out_specs=hbm,
        scratch_shapes=[
            pltpu.VMEM((per_band * band_count * 2 * support, LANES), bf16),
            pltpu.VMEM((count, LANES), f32),
            pltpu.VMEM((FIELDS, count + LANES), i32),
            pltpu.SMEM((FIELDS, count + LANES), i32),
            pltpu.VMEM((NCOL, 2 * rows), f32),
            pltpu.VMEM((UNROLL, rows, 2 * support), bf16),
            pltpu.VMEM((UNROLL, 2 * support, 2 * rows), bf16),
            pltpu.VMEM((UNROLL, 2 * support, 2 * support), bf16),
            pltpu.VMEM((NCOL // LANES, 2, rows, LANES), f32),
            pltpu.SemaphoreType.DMA(()),
            pltpu.SemaphoreType.DMA((NCOL // LANES,)),
        ],
        compiler_params=grant,
    )(*pieces, *screen_parts, *tables)


def solution(mesh):
    in_specs = (
        P("band", None, None, None),
        P(("grp", "band", "sub", "kern"), None, None),
        P(("grp", "band", "sub", "kern"), None),
        P(("grp", "band", "sub", "kern"), None),
        P(("grp", "band", "sub", "kern")),
        P(("grp", "band", "sub", "kern"), None),
        P(("grp", "band", "sub", "kern")),
        P(("grp", "band", "sub", "kern")),
    )
    out_specs = P(None, ("grp", "band", "sub", "kern"), None)
    return jax.shard_map(body, mesh=mesh, in_specs=in_specs, out_specs=out_specs, check_vma=False)
```

```python
import functools
import math

import jax
import jax.numpy as jnp
import numpy as np
from jax import lax
from jax.experimental import pallas as pl
from jax.experimental.pallas import tpu as pltpu
from jax.sharding import PartitionSpec as P


OVERS = 8
BR = 256
NCOL = 1024
LANES = 128
FIELDS = 8
UNROLL = 60
DIRECT_MOST = 4
VMEM_GRANT = 24 * 1024 * 1024

f32, bf16, i32 = jnp.float32, jnp.bfloat16, jnp.int32


def dft_tables(support):
    centred = np.arange(support, dtype=np.float32) - np.float32(support // 2)
    fractions = np.arange(OVERS, dtype=np.float32) / np.float32(OVERS)
    frequency = centred[None, :, None] + fractions[:, None, None]
    phases = np.float32(-2.0 * math.pi) * frequency * centred[None, None, :] / np.float32(support)
    scale = np.float32(support)
    return (
        (np.cos(phases) / scale).astype(jnp.bfloat16).astype(np.float32),
        (np.sin(phases) / scale).astype(jnp.bfloat16).astype(np.float32),
    )


def table_constants(support, rows):
    real, imag = dft_tables(support)
    padded = np.zeros((OVERS, support + 2 * rows, 2 * support), np.float32)
    padded[:, rows : rows + support] = np.concatenate([real, imag], axis=2)
    top = np.concatenate([real, -imag], axis=2)
    low = np.concatenate([imag, real], axis=2)
    columns = np.concatenate([top, low], axis=1).astype(jnp.bfloat16)
    return padded.reshape(-1, 2 * support), columns


def in_hbm(array):
    return pltpu.with_memory_space_constraint(array, pltpu.HBM)


def iota(shape, axis):
    return lax.broadcasted_iota(i32, shape, axis)


def nt_dot(left, right):
    return lax.dot_general(left, right, (((1,), (1,)), ((), ())), preferred_element_type=f32)


def nn_dot(left, right):
    return jnp.dot(left, right, preferred_element_type=f32)


def send_kernel(
    band_count, splits, capacity, direct,
    *refs,
):
    sources, outs, held = refs[:8], refs[8:-10], refs[-10:-2]
    line_ref, sems = refs[-2:]
    share, _, support, _ = held[0].shape
    first = lax.axis_index("kern") * share if splits > 1 else 0
    copies = []
    for index in (3, 4, 5, 6, 7, 2, 1, 0):
        source = sources[index].at[pl.ds(first, share)] if index == 0 else sources[index]
        copies.append(pltpu.make_async_copy(source, held[index], sems.at[index]))
    for copy in copies:
        copy.start()
    screens, values, columns, route, choice, offsets, row_cell, col_cell = held
    blocks, width = columns.shape
    me = lax.axis_index("band")
    for copy in copies[:5]:
        copy.wait()
    target = route[...]
    slots = band_count * capacity
    match = (iota((band_count, blocks), 0) == target).astype(f32)
    earlier = (iota((blocks, blocks), 0) < iota((blocks, blocks), 1)).astype(f32).astype(bf16)
    before = nn_dot(match.astype(bf16), earlier)
    rank = jnp.sum(before * match, axis=0, keepdims=True).astype(i32)
    slot = target * capacity + rank
    pick = (iota((slots, blocks), 0) == slot).astype(f32).astype(bf16)
    column = col_cell[...]
    fields = [
        choice[...], offsets[pl.ds(0, 1), :], offsets[pl.ds(1, 1), :], row_cell[...],
        column // LANES, column % LANES, jnp.ones_like(column), jnp.zeros_like(column),
    ]
    field_at = iota((FIELDS, blocks), 0)
    table = jnp.zeros((FIELDS, blocks), i32)
    for index, field in enumerate(fields):
        table = jnp.where(field_at == index, field, table)
    spread = (iota((FIELDS, LANES), 0) == iota((FIELDS, LANES), 1)).astype(f32).astype(bf16)
    meta = nt_dot(pick, table.astype(f32).astype(bf16)).astype(bf16)
    for copy in copies[5:]:
        copy.wait()
    for block in range(blocks):
        hits = iota((support, width), 0) == columns[pl.ds(block, 1), :]
        line = nt_dot(values[block], hits.astype(f32).astype(bf16))
        line_ref[0, pl.ds(block, 1), :] = line[0:1]
        line_ref[1, pl.ds(block, 1), :] = line[1:2]
    at_row, at_lane = iota((support, LANES), 0), iota((support, LANES), 1)
    place_re = (at_lane == (LANES - at_row) % LANES).astype(f32).astype(bf16)
    place_im = (at_lane == support - at_row).astype(f32).astype(bf16)
    lines = nn_dot(line_ref[0].astype(bf16), place_re) + nn_dot(line_ref[1].astype(bf16), place_im)
    payload = jnp.concatenate(
        [nn_dot(pick, lines.astype(bf16)), nn_dot(meta, spread)], axis=1
    )
    slot_ref = outs[-1]
    slot_ref[...] = payload
    outs = outs[:-1] if direct else [outs[0].at[step] for step in range(band_count)]
    for step, out in enumerate(outs):
        dest = partner(me, step, band_count) if direct else step
        mine = slot_ref[pl.ds(dest * capacity, capacity), :]
        out[pl.ds(0, capacity), :] = mine[:, :LANES].astype(bf16)
        out[pl.ds(capacity, capacity), :] = mine[:, LANES:].astype(bf16)
    for index in range(share):
        both = jnp.concatenate(
            [screens[index, 0].astype(f32), screens[index, 1].astype(f32)], axis=1
        ).astype(bf16)
        for out in outs:
            out[pl.ds(2 * capacity + index * support, support), :] = both


def partner(me, step, count):
    if count & (count - 1) == 0:
        return me ^ step
    return lax.rem(me + step, count)


def grid_kernel(
    band_count, kern_count, splits, held, deep, per_band, rows, support, direct, parts_of, *refs
):
    pieces, screen_parts = refs[: parts_of[0]], refs[parts_of[0] : parts_of[1]]
    row_tables, column_tables, out = refs[parts_of[1] : parts_of[1] + 3]
    screen_ref, line_ref, meta_vmem, meta_smem, total, half_ref, kernel_ref, skew_ref, stage, sem, sems = (
        refs[parts_of[1] + 3 :]
    )
    share = per_band // splits
    slices = [(piece, at) for piece in pieces for at in range(piece.shape[0])]
    lines = jnp.concatenate([piece[at, :held, :] for piece, at in slices], axis=0)
    metas = jnp.concatenate([piece[at, held : 2 * held, :] for piece, at in slices], axis=0)
    count = lines.shape[0]
    spread = (iota((FIELDS, LANES), 0) == iota((FIELDS, LANES), 1)).astype(f32).astype(bf16)
    fields = nt_dot(spread, metas)
    kern = lax.axis_index("kern")
    low = ((lax.axis_index("sub") * kern_count + kern) * rows).astype(f32)
    row_at = fields[3:4]
    live = (fields[6:7] > 0.5) & (row_at < low + rows) & (row_at + support > low)
    live = live.astype(f32)
    upper = (iota((count, count), 0) < iota((count, count), 1)).astype(f32).astype(bf16)
    rank = nn_dot(jnp.broadcast_to(live, (FIELDS, count)).astype(bf16), upper)[0:1]
    start = (low + rows - row_at) * live
    field_at = iota((FIELDS, count), 0)
    packed = jnp.where(field_at == 3, start, fields) * live
    pick = (iota((count, count), 0).astype(f32) == rank).astype(f32) * live
    pick = pick.astype(bf16)
    line_ref[pl.ds(0, count), :] = nn_dot(pick, lines)
    line_ref[pl.ds(count, LANES), :] = jnp.zeros((LANES, LANES), f32)
    chosen = nt_dot(packed.astype(bf16), pick)
    number = jnp.sum(live)
    screen = chosen[0:1].astype(i32)
    sizes = [screen_ref.shape[0] // (2 * support), row_tables.shape[0], OVERS]
    bits = [(size - 1).bit_length() for size in sizes]
    shifts = [sum(bits[: at + 1]) for at in range(3)]
    assert shifts[-1] + (NCOL - 1).bit_length() < 32
    me = lax.axis_index("band")
    band_of = screen // per_band
    if not direct:
        step_of = band_of
    elif band_count & (band_count - 1) == 0:
        step_of = band_of ^ me
    else:
        step_of = (band_of - me + band_count) % band_count
    within = screen % per_band
    place = step_of * share + within % share
    if splits > 1:
        place = place + ((within // share) != kern).astype(i32) * (band_count * share)
    table_row = chosen[1:2].astype(i32) * (support + 2 * rows) + chosen[3:4].astype(i32)
    col = chosen[4:5].astype(i32) * LANES + chosen[5:6].astype(i32)
    word = place
    for shift, field in zip(shifts, (table_row, chosen[2:3].astype(i32), col)):
        word = word + field * (1 << shift)
    meta_vmem[:, pl.ds(0, count)] = word
    meta_vmem[:, pl.ds(count, LANES)] = jnp.broadcast_to(number.astype(i32), (1, LANES))
    copy = pltpu.make_async_copy(meta_vmem, meta_smem, sem)
    copy.start()
    lane = iota((support, LANES), 1)
    sign = jnp.where(lane < support, -1.0, 1.0).astype(f32)
    span = NCOL // band_count

    def unfold(step, carry):
        for part_at, part in enumerate(screen_parts):
            for index in range(share):
                both = part[step, pl.ds(deep + index * support, support), :]
                turned = pltpu.roll(both.astype(f32), support, 1) * sign
                at = ((part_at * band_count + step) * share + index) * 2 * support
                at = pl.multiple_of(at, 2 * support)
                screen_ref[pl.ds(at, support), :] = both
                screen_ref[pl.ds(at + support, support), :] = turned.astype(bf16)
        total[pl.ds(pl.multiple_of(step * span, span), span), :] = jnp.zeros((span, 2 * rows), f32)
        return carry

    lax.fori_loop(0, band_count, unfold, 0)
    y_at, l_at = iota((2 * support, LANES), 0), iota((2 * support, LANES), 1)
    lag = y_at - l_at % support
    keep = ((lag >= 0) & (lag < support)).astype(f32).astype(bf16)
    wide = 2 * support
    copy.wait()

    def part_of(word, at):
        lower = shifts[at - 1] if at else 0
        high = word >> lower
        return high & ((1 << bits[at]) - 1) if at < 3 else high

    def turn(index, carry):
        ids = [index * UNROLL + extra for extra in range(UNROLL)]
        words = [meta_smem[0, k] for k in ids]
        for at, word in enumerate(words):
            left = row_tables[pl.ds(part_of(word, 1), rows), :].astype(bf16)
            screen_at = pl.multiple_of(part_of(word, 0) * wide, wide)
            right = screen_ref[pl.ds(screen_at, wide), :]
            half_ref[at] = nn_dot(left, right).astype(bf16)
        for at, k in enumerate(ids):
            line = jnp.broadcast_to(line_ref[pl.ds(k, 1), :], (wide, LANES))
            skew_ref[at] = pltpu.roll(line, 0, 1, stride=1, stride_axis=0).astype(bf16) * keep
        for at, word in enumerate(words):
            both = nt_dot(column_tables[part_of(word, 2)], half_ref[at]).astype(bf16)
            real, imag = both[:support], both[support:]
            kernel_ref[at, pl.ds(0, support), :] = jnp.concatenate([real, imag], axis=1)
            kernel_ref[at, pl.ds(support, support), :] = jnp.concatenate([-imag, real], axis=1)
        for at, word in enumerate(words):
            window = pl.ds(part_of(word, 3), wide)
            total[window, :] = total[window, :] + nn_dot(skew_ref[at], kernel_ref[at])
        return carry

    turns = (meta_smem[0, count] + (UNROLL - 1)) // UNROLL
    lax.fori_loop(0, turns, turn, 0)
    writes = []
    for at in range(NCOL // LANES):
        turned = total[pl.ds(at * LANES, LANES), :].T
        stage[at, 0] = turned[:rows]
        stage[at, 1] = turned[rows:]
        target = out.at[:, :, pl.ds(at * LANES, LANES)]
        writes.append(pltpu.make_async_copy(stage.at[at], target, sems.at[at]))
        writes[-1].start()
    for write in writes:
        write.wait()


def table_kernel(row_source, column_source, row_tables, column_tables, sems):
    copies = [
        pltpu.make_async_copy(row_source, row_tables, sems.at[0]),
        pltpu.make_async_copy(column_source, column_tables, sems.at[1]),
    ]
    for copy in copies:
        copy.start()
    for copy in copies:
        copy.wait()


def exchange(parts, axis, count):
    if count & (count - 1) == 0:
        perms = [[(i, i ^ step) for i in range(count)] for step in range(count)]
    else:
        perms = [[((i + step) % count, i) for i in range(count)] for step in range(count)]
    return [parts[0]] + [lax.ppermute(parts[step], axis, perms[step]) for step in range(1, count)]


def program(
    screens, visibilities, vis_columns, band_route, screen_choice, offsets, row_cell, col_cell
):
    band_count = lax.axis_size("band")
    sub_count, kern_count = lax.axis_size("sub"), lax.axis_size("kern")
    per_band, _, support, _ = screens.shape
    blocks = visibilities.shape[0]
    capacity = 2 * blocks // band_count
    rows = BR // (sub_count * kern_count)
    members = sub_count * kern_count
    group = ("sub", "kern")
    direct = band_count <= DIRECT_MOST and members in (1, 2, 4)
    splits = 2 if kern_count == 2 and per_band % 2 == 0 else 1
    share = per_band // splits
    depth = 2 * capacity + share * support
    vmem = pl.BlockSpec(memory_space=pltpu.VMEM)
    hbm = pl.BlockSpec(memory_space=pltpu.HBM)
    grant = pltpu.CompilerParams(vmem_limit_bytes=VMEM_GRANT)
    if direct:
        messages = [jax.ShapeDtypeStruct((depth, LANES), bf16)] * band_count
    else:
        messages = [jax.ShapeDtypeStruct((band_count, depth, LANES), bf16)]
    sent = pl.pallas_call(
        functools.partial(send_kernel, band_count, splits, capacity, direct),
        out_shape=messages + [jax.ShapeDtypeStruct((band_count * capacity, 2 * LANES), f32)],
        in_specs=[hbm] * 8,
        out_specs=[vmem] * (len(messages) + 1),
        scratch_shapes=[
            pltpu.VMEM((share,) + screens.shape[1:], bf16),
            pltpu.VMEM(visibilities.shape, bf16),
            pltpu.VMEM(vis_columns.shape, i32),
            pltpu.VMEM((1, blocks), i32),
            pltpu.VMEM((1, blocks), i32),
            pltpu.VMEM((2, blocks), i32),
            pltpu.VMEM((1, blocks), i32),
            pltpu.VMEM((1, blocks), i32),
            pltpu.VMEM((2, blocks, support), f32),
            pltpu.SemaphoreType.DMA((8,)),
        ],
        compiler_params=grant,
    )(
        *map(
            in_hbm,
            (
                screens, visibilities, vis_columns, band_route.reshape(1, blocks),
                screen_choice.reshape(1, blocks), offsets.T, row_cell.reshape(1, blocks),
                col_cell.reshape(1, blocks),
            ),
        )
    )
    count = members * band_count * capacity
    if direct:
        own = jnp.stack(exchange(sent[:-1], "band", band_count))
        slots = own[:, : 2 * capacity]
        pieces, screen_parts, held, deep = [own], [own], capacity, 2 * capacity
        for step in range(1, members):
            whole = splits > 1 and step == 1
            perm = [(i, i ^ step) for i in range(members)]
            got = lax.ppermute(own if whole else slots, group, perm)
            pieces.append(got)
            if whole:
                screen_parts.append(got)
    else:
        own = lax.all_to_all(sent[0], "band", 0, 0, tiled=True)
        slots = lax.all_gather(own[:, : 2 * capacity], group, axis=0, tiled=True)
        slots = slots.reshape(members * band_count, 2, capacity, LANES)
        pieces = [slots.transpose(1, 0, 2, 3).reshape(1, 2 * count, LANES)]
        screen_parts, held, deep = [own[:, 2 * capacity :]], count, 0
        if splits > 1:
            perm = [(i, i ^ 1) for i in range(kern_count)]
            screen_parts.append(lax.ppermute(screen_parts[0], "kern", perm))
    tables = [jnp.asarray(table) for table in table_constants(support, rows)]
    tables = pl.pallas_call(
        table_kernel,
        out_shape=[jax.ShapeDtypeStruct(table.shape, table.dtype) for table in tables],
        in_specs=[hbm] * 2,
        out_specs=[vmem] * 2,
        scratch_shapes=[pltpu.SemaphoreType.DMA((2,))],
        compiler_params=grant,
        cost_estimate=pl.CostEstimate(flops=0, bytes_accessed=1 << 21, transcendentals=0),
    )(*map(in_hbm, tables))
    parts_of = (len(pieces), len(pieces) + len(screen_parts))
    return pl.pallas_call(
        functools.partial(
            grid_kernel, band_count, kern_count, splits, held, deep, per_band, rows, support,
            direct, parts_of,
        ),
        out_shape=jax.ShapeDtypeStruct((2, rows, NCOL), f32),
        in_specs=[vmem] * (parts_of[1] + 2),
        out_specs=hbm,
        scratch_shapes=[
            pltpu.VMEM((per_band * band_count * 2 * support, LANES), bf16),
            pltpu.VMEM((count + LANES, LANES), f32),
            pltpu.VMEM((1, count + LANES), i32),
            pltpu.SMEM((1, count + LANES), i32),
            pltpu.VMEM((NCOL, 2 * rows), f32),
            pltpu.VMEM((UNROLL, rows, 2 * support), bf16),
            pltpu.VMEM((UNROLL, 2 * support, 2 * rows), bf16),
            pltpu.VMEM((UNROLL, 2 * support, 2 * support), bf16),
            pltpu.VMEM((NCOL // LANES, 2, rows, LANES), f32),
            pltpu.SemaphoreType.DMA(()),
            pltpu.SemaphoreType.DMA((NCOL // LANES,)),
        ],
        compiler_params=grant,
    )(*pieces, *screen_parts, *tables)


def solution(mesh):
    in_specs = (
        P("band", None, None, None),
        P(("grp", "band", "sub", "kern"), None, None),
        P(("grp", "band", "sub", "kern"), None),
        P(("grp", "band", "sub", "kern"), None),
        P(("grp", "band", "sub", "kern")),
        P(("grp", "band", "sub", "kern"), None),
        P(("grp", "band", "sub", "kern")),
        P(("grp", "band", "sub", "kern")),
    )
    out_specs = P(None, ("grp", "band", "sub", "kern"), None)
    return jax.shard_map(program, mesh=mesh, in_specs=in_specs, out_specs=out_specs, check_vma=False)
```

```python
import functools
import math

import jax
import jax.numpy as jnp
import numpy as np
from jax import lax
from jax.experimental import pallas as pl
from jax.experimental.pallas import tpu as pltpu
from jax.sharding import PartitionSpec as P


OVERS = 8
BR = 256
NCOL = 1024
LANES = 128
FIELDS = 8
UNROLL = 60
DIRECT_MOST = 4
VMEM_GRANT = 24 * 1024 * 1024

f32, bf16, i32 = jnp.float32, jnp.bfloat16, jnp.int32


def dft_tables(support):
    centred = np.arange(support, dtype=np.float32) - np.float32(support // 2)
    fractions = np.arange(OVERS, dtype=np.float32) / np.float32(OVERS)
    frequency = centred[None, :, None] + fractions[:, None, None]
    phases = np.float32(-2.0 * math.pi) * frequency * centred[None, None, :] / np.float32(support)
    scale = np.float32(support)
    return (
        (np.cos(phases) / scale).astype(jnp.bfloat16).astype(np.float32),
        (np.sin(phases) / scale).astype(jnp.bfloat16).astype(np.float32),
    )


def table_constants(support, rows):
    real, imag = dft_tables(support)
    padded = np.zeros((OVERS, support + 2 * rows, 2 * support), np.float32)
    padded[:, rows : rows + support] = np.concatenate([real, imag], axis=2)
    top = np.concatenate([real, -imag], axis=2)
    low = np.concatenate([imag, real], axis=2)
    columns = np.concatenate([top, low], axis=1).astype(jnp.bfloat16)
    return padded.reshape(-1, 2 * support), columns


def in_hbm(array):
    return pltpu.with_memory_space_constraint(array, pltpu.HBM)


def iota(shape, axis):
    return lax.broadcasted_iota(i32, shape, axis)


def nt_dot(left, right):
    return lax.dot_general(left, right, (((1,), (1,)), ((), ())), preferred_element_type=f32)


def nn_dot(left, right):
    return jnp.dot(left, right, preferred_element_type=f32)


def send_kernel(
    band_count, splits, capacity, fold, direct,
    *refs,
):
    sources, outs, held = refs[:8], refs[8:-11], refs[-11:-3]
    line_ref, slot_ref, sems = refs[-3:]
    share, _, support, _ = held[0].shape
    first = lax.axis_index("kern") * share if splits > 1 else 0
    copies = []
    for index in (3, 4, 5, 6, 7, 2, 1, 0):
        source = sources[index].at[pl.ds(first, share)] if index == 0 else sources[index]
        copies.append(pltpu.make_async_copy(source, held[index], sems.at[index]))
    for copy in copies:
        copy.start()
    screens, values, columns, route, choice, offsets, row_cell, col_cell = held
    blocks, width = columns.shape
    me = lax.axis_index("band")
    for copy in copies[:5]:
        copy.wait()
    target = route[...]
    slots = band_count * capacity
    match = (iota((band_count, blocks), 0) == target).astype(f32)
    earlier = (iota((blocks, blocks), 0) < iota((blocks, blocks), 1)).astype(f32).astype(bf16)
    before = nn_dot(match.astype(bf16), earlier)
    rank = jnp.sum(before * match, axis=0, keepdims=True).astype(i32)
    slot = target * capacity + rank
    pick = (iota((slots, blocks), 0) == slot).astype(f32).astype(bf16)
    column = col_cell[...]
    fields = [
        choice[...], offsets[pl.ds(0, 1), :], offsets[pl.ds(1, 1), :], row_cell[...],
        column // LANES, column % LANES, jnp.ones_like(column), jnp.zeros_like(column),
    ]
    field_at = iota((FIELDS, blocks), 0)
    table = jnp.zeros((FIELDS, blocks), i32)
    for index, field in enumerate(fields):
        table = jnp.where(field_at == index, field, table)
    spread = (iota((FIELDS, LANES), 0) == iota((FIELDS, LANES), 1)).astype(f32).astype(bf16)
    meta = nt_dot(pick, table.astype(f32).astype(bf16)).astype(bf16)
    for copy in copies[5:]:
        copy.wait()
    for block in range(blocks):
        hits = iota((support, width), 0) == columns[pl.ds(block, 1), :]
        line = nt_dot(values[block], hits.astype(f32).astype(bf16))
        line_ref[0, pl.ds(block, 1), :] = line[0:1]
        line_ref[1, pl.ds(block, 1), :] = line[1:2]
    at_row, at_lane = iota((support, LANES), 0), iota((support, LANES), 1)
    place_re = (at_lane == (LANES - at_row) % LANES).astype(f32).astype(bf16)
    place_im = (at_lane == support - at_row).astype(f32).astype(bf16)
    lines = nn_dot(line_ref[0].astype(bf16), place_re) + nn_dot(line_ref[1].astype(bf16), place_im)
    payload = jnp.concatenate(
        [nn_dot(pick, lines.astype(bf16)), nn_dot(meta, spread)], axis=1
    )
    slot_ref[...] = payload
    outs = outs if direct else [outs[0].at[step] for step in range(band_count)]
    for step, out in enumerate(outs):
        dest = partner(me, step, band_count) if direct else step
        mine = slot_ref[pl.ds(dest * capacity, capacity), :]
        out[pl.ds(0, capacity), :] = mine[:, :LANES].astype(bf16)
        part = capacity // fold
        metas = mine[:part, LANES:]
        if fold > 1:
            metas = metas + pltpu.roll(mine[part:, LANES:], LANES // 2, 1)
        out[pl.ds(capacity, part), :] = metas.astype(bf16)
    for index in range(share):
        both = jnp.concatenate(
            [screens[index, 0].astype(f32), screens[index, 1].astype(f32)], axis=1
        ).astype(bf16)
        for out in outs:
            out[pl.ds(capacity + capacity // fold + index * support, support), :] = both


def partner(me, step, count):
    if count & (count - 1) == 0:
        return me ^ step
    return lax.rem(me + step, count)


def grid_kernel(
    band_count, kern_count, splits, held, fold, deep, per_band, rows, support, direct, parts_of, *refs
):
    pieces, screen_parts = refs[: parts_of[0]], refs[parts_of[0] : parts_of[1]]
    row_tables, column_tables, out = refs[parts_of[1] : parts_of[1] + 3]
    screen_ref, line_ref, meta_vmem, meta_smem, total, half_ref, kernel_ref, skew_ref, stage, sem, sems = (
        refs[parts_of[1] + 3 :]
    )
    share = per_band // splits
    slices = [(piece, at) for piece in pieces for at in range(piece.shape[0])]
    part = held // fold
    lines = jnp.concatenate(
        [piece[at, turn * part : (turn + 1) * part, :] for turn in range(fold) for piece, at in slices],
        axis=0,
    )
    metas = jnp.concatenate([piece[at, held : held + part, :] for piece, at in slices], axis=0)
    count = lines.shape[0]
    f_at, f_lane = iota((FIELDS, LANES), 0), iota((FIELDS, LANES), 1)
    spreads = [(f_lane == f_at + turn * (LANES // 2)).astype(f32).astype(bf16) for turn in range(fold)]
    fields = jnp.concatenate([nt_dot(spread, metas) for spread in spreads], axis=1)
    kern = lax.axis_index("kern")
    low = ((lax.axis_index("sub") * kern_count + kern) * rows).astype(f32)
    row_at = fields[3:4]
    live = (fields[6:7] > 0.5) & (row_at < low + rows) & (row_at + support > low)
    live = live.astype(f32)
    upper = (iota((count, count), 0) < iota((count, count), 1)).astype(f32).astype(bf16)
    rank = nn_dot(jnp.broadcast_to(live, (FIELDS, count)).astype(bf16), upper)[0:1]
    start = (low + rows - row_at) * live
    field_at = iota((FIELDS, count), 0)
    packed = jnp.where(field_at == 3, start, fields) * live
    pick = (iota((count, count), 0).astype(f32) == rank).astype(f32) * live
    pick = pick.astype(bf16)
    line_ref[pl.ds(0, count), :] = nn_dot(pick, lines)
    line_ref[pl.ds(count, LANES), :] = jnp.zeros((LANES, LANES), f32)
    chosen = nt_dot(packed.astype(bf16), pick)
    number = jnp.sum(live)
    screen = chosen[0:1].astype(i32)
    sizes = [screen_ref.shape[0] // (2 * support), row_tables.shape[0], OVERS]
    bits = [(size - 1).bit_length() for size in sizes]
    shifts = [sum(bits[: at + 1]) for at in range(3)]
    assert shifts[-1] + (NCOL - 1).bit_length() < 32
    me = lax.axis_index("band")
    band_of = screen // per_band
    if not direct:
        step_of = band_of
    elif band_count & (band_count - 1) == 0:
        step_of = band_of ^ me
    else:
        step_of = (band_of - me + band_count) % band_count
    within = screen % per_band
    place = step_of * share + within % share
    if splits > 1:
        place = place + ((within // share) != kern).astype(i32) * (band_count * share)
    table_row = chosen[1:2].astype(i32) * (support + 2 * rows) + chosen[3:4].astype(i32)
    col = chosen[4:5].astype(i32) * LANES + chosen[5:6].astype(i32)
    word = place
    for shift, field in zip(shifts, (table_row, chosen[2:3].astype(i32), col)):
        word = word + field * (1 << shift)
    meta_vmem[:, pl.ds(0, count)] = word
    meta_vmem[:, pl.ds(count, LANES)] = jnp.broadcast_to(number.astype(i32), (1, LANES))
    copy = pltpu.make_async_copy(meta_vmem, meta_smem, sem)
    copy.start()
    lane = iota((support, LANES), 1)
    sign = jnp.where(lane < support, -1.0, 1.0).astype(f32)
    span = NCOL // band_count

    def unfold(step, carry):
        for part_at, part in enumerate(screen_parts):
            for index in range(share):
                both = part[step, pl.ds(deep + index * support, support), :]
                turned = pltpu.roll(both.astype(f32), support, 1) * sign
                at = ((part_at * band_count + step) * share + index) * 2 * support
                at = pl.multiple_of(at, 2 * support)
                screen_ref[pl.ds(at, support), :] = both
                screen_ref[pl.ds(at + support, support), :] = turned.astype(bf16)
        total[pl.ds(pl.multiple_of(step * span, span), span), :] = jnp.zeros((span, 2 * rows), f32)
        return carry

    lax.fori_loop(0, band_count, unfold, 0)
    y_at, l_at = iota((2 * support, LANES), 0), iota((2 * support, LANES), 1)
    lag = y_at - l_at % support
    keep = ((lag >= 0) & (lag < support)).astype(f32).astype(bf16)
    wide = 2 * support
    copy.wait()

    def part_of(word, at):
        lower = shifts[at - 1] if at else 0
        high = word >> lower
        return high & ((1 << bits[at]) - 1) if at < 3 else high

    def turn(index, carry):
        ids = [index * UNROLL + extra for extra in range(UNROLL)]
        words = [meta_smem[0, k] for k in ids]
        for at, word in enumerate(words):
            left = row_tables[pl.ds(part_of(word, 1), rows), :].astype(bf16)
            screen_at = pl.multiple_of(part_of(word, 0) * wide, wide)
            right = screen_ref[pl.ds(screen_at, wide), :]
            half_ref[at] = nn_dot(left, right).astype(bf16)
        for at, k in enumerate(ids):
            line = jnp.broadcast_to(line_ref[pl.ds(k, 1), :], (wide, LANES))
            skew_ref[at] = pltpu.roll(line, 0, 1, stride=1, stride_axis=0).astype(bf16) * keep
        for at, word in enumerate(words):
            both = nt_dot(column_tables[part_of(word, 2)], half_ref[at]).astype(bf16)
            real, imag = both[:support], both[support:]
            kernel_ref[at, pl.ds(0, support), :] = jnp.concatenate([real, imag], axis=1)
            kernel_ref[at, pl.ds(support, support), :] = jnp.concatenate([-imag, real], axis=1)
        for at, word in enumerate(words):
            window = pl.ds(part_of(word, 3), wide)
            total[window, :] = total[window, :] + nn_dot(skew_ref[at], kernel_ref[at])
        return carry

    turns = (meta_smem[0, count] + (UNROLL - 1)) // UNROLL
    lax.fori_loop(0, turns, turn, 0)
    writes = []
    for at in range(NCOL // LANES):
        turned = total[pl.ds(at * LANES, LANES), :].T
        stage[at, 0] = turned[:rows]
        stage[at, 1] = turned[rows:]
        target = out.at[:, :, pl.ds(at * LANES, LANES)]
        writes.append(pltpu.make_async_copy(stage.at[at], target, sems.at[at]))
        writes[-1].start()
    for write in writes:
        write.wait()


def table_kernel(row_source, column_source, row_tables, column_tables, sems):
    copies = [
        pltpu.make_async_copy(row_source, row_tables, sems.at[0]),
        pltpu.make_async_copy(column_source, column_tables, sems.at[1]),
    ]
    for copy in copies:
        copy.start()
    for copy in copies:
        copy.wait()


def exchange(parts, axis, count):
    if count & (count - 1) == 0:
        perms = [[(i, i ^ step) for i in range(count)] for step in range(count)]
    else:
        perms = [[((i + step) % count, i) for i in range(count)] for step in range(count)]
    return [parts[0]] + [lax.ppermute(parts[step], axis, perms[step]) for step in range(1, count)]


def program(
    screens, visibilities, vis_columns, band_route, screen_choice, offsets, row_cell, col_cell
):
    band_count = lax.axis_size("band")
    sub_count, kern_count = lax.axis_size("sub"), lax.axis_size("kern")
    per_band, _, support, _ = screens.shape
    blocks = visibilities.shape[0]
    capacity = 2 * blocks // band_count
    rows = BR // (sub_count * kern_count)
    members = sub_count * kern_count
    group = ("sub", "kern")
    direct = band_count <= DIRECT_MOST and members in (1, 2, 4)
    splits = 2 if kern_count == 2 and per_band % 2 == 0 else 1
    share = per_band // splits
    fold = 2 if direct and capacity % 16 == 0 else 1
    top = capacity + capacity // fold
    depth = top + share * support
    vmem = pl.BlockSpec(memory_space=pltpu.VMEM)
    hbm = pl.BlockSpec(memory_space=pltpu.HBM)
    grant = pltpu.CompilerParams(vmem_limit_bytes=VMEM_GRANT)
    if direct:
        messages = [jax.ShapeDtypeStruct((depth, LANES), bf16)] * band_count
    else:
        messages = [jax.ShapeDtypeStruct((band_count, depth, LANES), bf16)]
    sent = pl.pallas_call(
        functools.partial(send_kernel, band_count, splits, capacity, fold, direct),
        out_shape=messages,
        in_specs=[hbm] * 8,
        out_specs=[vmem] * len(messages),
        scratch_shapes=[
            pltpu.VMEM((share,) + screens.shape[1:], bf16),
            pltpu.VMEM(visibilities.shape, bf16),
            pltpu.VMEM(vis_columns.shape, i32),
            pltpu.VMEM((1, blocks), i32),
            pltpu.VMEM((1, blocks), i32),
            pltpu.VMEM((2, blocks), i32),
            pltpu.VMEM((1, blocks), i32),
            pltpu.VMEM((1, blocks), i32),
            pltpu.VMEM((2, blocks, support), f32),
            pltpu.VMEM((band_count * capacity, 2 * LANES), f32),
            pltpu.SemaphoreType.DMA((8,)),
        ],
        compiler_params=grant,
    )(
        *map(
            in_hbm,
            (
                screens, visibilities, vis_columns, band_route.reshape(1, blocks),
                screen_choice.reshape(1, blocks), offsets.T, row_cell.reshape(1, blocks),
                col_cell.reshape(1, blocks),
            ),
        )
    )
    count = members * band_count * capacity
    if direct:
        own = jnp.stack(exchange(sent, "band", band_count))
        slots = own[:, :top]
        pieces, screen_parts, held, deep = [own], [own], capacity, top
        for step in range(1, members):
            whole = splits > 1 and step == 1
            perm = [(i, i ^ step) for i in range(members)]
            got = lax.ppermute(own if whole else slots, group, perm)
            pieces.append(got)
            if whole:
                screen_parts.append(got)
    else:
        own = lax.all_to_all(sent[0], "band", 0, 0, tiled=True)
        slots = lax.all_gather(own[:, : 2 * capacity], group, axis=0, tiled=True)
        slots = slots.reshape(members * band_count, 2, capacity, LANES)
        pieces = [slots.transpose(1, 0, 2, 3).reshape(1, 2 * count, LANES)]
        screen_parts, held, deep = [own[:, 2 * capacity :]], count, 0
        if splits > 1:
            perm = [(i, i ^ 1) for i in range(kern_count)]
            screen_parts.append(lax.ppermute(screen_parts[0], "kern", perm))
    tables = [jnp.asarray(table) for table in table_constants(support, rows)]
    tables = pl.pallas_call(
        table_kernel,
        out_shape=[jax.ShapeDtypeStruct(table.shape, table.dtype) for table in tables],
        in_specs=[hbm] * 2,
        out_specs=[vmem] * 2,
        scratch_shapes=[pltpu.SemaphoreType.DMA((2,))],
        compiler_params=grant,
        cost_estimate=pl.CostEstimate(flops=0, bytes_accessed=1 << 21, transcendentals=0),
    )(*map(in_hbm, tables))
    parts_of = (len(pieces), len(pieces) + len(screen_parts))
    return pl.pallas_call(
        functools.partial(
            grid_kernel, band_count, kern_count, splits, held, fold, deep, per_band, rows, support,
            direct, parts_of,
        ),
        out_shape=jax.ShapeDtypeStruct((2, rows, NCOL), f32),
        in_specs=[vmem] * (parts_of[1] + 2),
        out_specs=hbm,
        scratch_shapes=[
            pltpu.VMEM((per_band * band_count * 2 * support, LANES), bf16),
            pltpu.VMEM((count + LANES, LANES), f32),
            pltpu.VMEM((1, count + LANES), i32),
            pltpu.SMEM((1, count + LANES), i32),
            pltpu.VMEM((NCOL, 2 * rows), f32),
            pltpu.VMEM((UNROLL, rows, 2 * support), bf16),
            pltpu.VMEM((UNROLL, 2 * support, 2 * rows), bf16),
            pltpu.VMEM((UNROLL, 2 * support, 2 * support), bf16),
            pltpu.VMEM((NCOL // LANES, 2, rows, LANES), f32),
            pltpu.SemaphoreType.DMA(()),
            pltpu.SemaphoreType.DMA((NCOL // LANES,)),
        ],
        compiler_params=grant,
    )(*pieces, *screen_parts, *tables)


def solution(mesh):
    in_specs = (
        P("band", None, None, None),
        P(("grp", "band", "sub", "kern"), None, None),
        P(("grp", "band", "sub", "kern"), None),
        P(("grp", "band", "sub", "kern"), None),
        P(("grp", "band", "sub", "kern")),
        P(("grp", "band", "sub", "kern"), None),
        P(("grp", "band", "sub", "kern")),
        P(("grp", "band", "sub", "kern")),
    )
    out_specs = P(None, ("grp", "band", "sub", "kern"), None)
    return jax.shard_map(program, mesh=mesh, in_specs=in_specs, out_specs=out_specs, check_vma=False)
```

```python
import functools
import math

import jax
import jax.numpy as jnp
import numpy as np
from jax import lax
from jax.experimental import pallas as pl
from jax.experimental.pallas import tpu as pltpu
from jax.sharding import PartitionSpec as P


OVERS = 8
BR = 256
NCOL = 1024
LANES = 128
FIELDS = 8
UNROLL = 60
LAST_TURN = 48
DIRECT_MOST = 4
VMEM_GRANT = 24 * 1024 * 1024

f32, bf16, i32 = jnp.float32, jnp.bfloat16, jnp.int32


def dft_tables(support):
    centred = np.arange(support, dtype=np.float32) - np.float32(support // 2)
    fractions = np.arange(OVERS, dtype=np.float32) / np.float32(OVERS)
    frequency = centred[None, :, None] + fractions[:, None, None]
    phases = np.float32(-2.0 * math.pi) * frequency * centred[None, None, :] / np.float32(support)
    scale = np.float32(support)
    return (
        (np.cos(phases) / scale).astype(jnp.bfloat16).astype(np.float32),
        (np.sin(phases) / scale).astype(jnp.bfloat16).astype(np.float32),
    )


def table_constants(support, rows):
    real, imag = dft_tables(support)
    padded = np.zeros((OVERS, support + 2 * rows, 2 * support), np.float32)
    padded[:, rows : rows + support] = np.concatenate([real, imag], axis=2)
    top = np.concatenate([real, -imag], axis=2)
    low = np.concatenate([imag, real], axis=2)
    columns = np.concatenate([top, low], axis=1).astype(jnp.bfloat16)
    return padded.reshape(-1, 2 * support), columns


def in_hbm(array):
    return pltpu.with_memory_space_constraint(array, pltpu.HBM)


def iota(shape, axis):
    return lax.broadcasted_iota(i32, shape, axis)


def nt_dot(left, right):
    return lax.dot_general(left, right, (((1,), (1,)), ((), ())), preferred_element_type=f32)


def nn_dot(left, right):
    return jnp.dot(left, right, preferred_element_type=f32)


def send_kernel(
    band_count, splits, capacity, fold, direct,
    *refs,
):
    sources, outs, held = refs[:8], refs[8:-11], refs[-11:-3]
    line_ref, slot_ref, sems = refs[-3:]
    share, _, support, _ = held[0].shape
    first = lax.axis_index("kern") * share if splits > 1 else 0
    copies = []
    for index in (3, 4, 5, 6, 7, 2, 1, 0):
        source = sources[index].at[pl.ds(first, share)] if index == 0 else sources[index]
        copies.append(pltpu.make_async_copy(source, held[index], sems.at[index]))
    for copy in copies:
        copy.start()
    screens, values, columns, route, choice, offsets, row_cell, col_cell = held
    blocks, width = columns.shape
    me = lax.axis_index("band")
    for copy in copies[:5]:
        copy.wait()
    target = route[...]
    slots = band_count * capacity
    match = (iota((band_count, blocks), 0) == target).astype(f32)
    earlier = (iota((blocks, blocks), 0) < iota((blocks, blocks), 1)).astype(f32).astype(bf16)
    before = nn_dot(match.astype(bf16), earlier)
    rank = jnp.sum(before * match, axis=0, keepdims=True).astype(i32)
    slot = target * capacity + rank
    pick = (iota((slots, blocks), 0) == slot).astype(f32).astype(bf16)
    column = col_cell[...]
    fields = [
        choice[...], offsets[pl.ds(0, 1), :], offsets[pl.ds(1, 1), :], row_cell[...],
        column // LANES, column % LANES, jnp.ones_like(column), jnp.zeros_like(column),
    ]
    field_at = iota((FIELDS, blocks), 0)
    table = jnp.zeros((FIELDS, blocks), i32)
    for index, field in enumerate(fields):
        table = jnp.where(field_at == index, field, table)
    spread = (iota((FIELDS, LANES), 0) == iota((FIELDS, LANES), 1)).astype(f32).astype(bf16)
    meta = nt_dot(pick, table.astype(f32).astype(bf16)).astype(bf16)
    for copy in copies[5:]:
        copy.wait()
    for block in range(blocks):
        hits = iota((support, width), 0) == columns[pl.ds(block, 1), :]
        line = nt_dot(values[block], hits.astype(f32).astype(bf16))
        line_ref[0, pl.ds(block, 1), :] = line[0:1]
        line_ref[1, pl.ds(block, 1), :] = line[1:2]
    at_row, at_lane = iota((support, LANES), 0), iota((support, LANES), 1)
    place_re = (at_lane == (LANES - at_row) % LANES).astype(f32).astype(bf16)
    place_im = (at_lane == support - at_row).astype(f32).astype(bf16)
    lines = nn_dot(line_ref[0].astype(bf16), place_re) + nn_dot(line_ref[1].astype(bf16), place_im)
    payload = jnp.concatenate(
        [nn_dot(pick, lines.astype(bf16)), nn_dot(meta, spread)], axis=1
    )
    slot_ref[...] = payload
    outs = outs if direct else [outs[0].at[step] for step in range(band_count)]
    for step, out in enumerate(outs):
        dest = partner(me, step, band_count) if direct else step
        mine = slot_ref[pl.ds(dest * capacity, capacity), :]
        out[pl.ds(0, capacity), :] = mine[:, :LANES].astype(bf16)
        part = capacity // fold
        metas = mine[:part, LANES:]
        if fold > 1:
            metas = metas + pltpu.roll(mine[part:, LANES:], LANES // 2, 1)
        out[pl.ds(capacity, part), :] = metas.astype(bf16)
    for index in range(share):
        both = jnp.concatenate(
            [screens[index, 0].astype(f32), screens[index, 1].astype(f32)], axis=1
        ).astype(bf16)
        for out in outs:
            out[pl.ds(capacity + capacity // fold + index * support, support), :] = both


def partner(me, step, count):
    if count & (count - 1) == 0:
        return me ^ step
    return lax.rem(me + step, count)


def grid_kernel(
    band_count, kern_count, splits, held, fold, deep, per_band, rows, support, direct, parts_of, *refs
):
    pieces, screen_parts = refs[: parts_of[0]], refs[parts_of[0] : parts_of[1]]
    row_tables, column_tables, out = refs[parts_of[1] : parts_of[1] + 3]
    screen_ref, line_ref, meta_vmem, meta_smem, total, half_ref, kernel_ref, skew_ref, stage, sem, sems = (
        refs[parts_of[1] + 3 :]
    )
    share = per_band // splits
    slices = [(piece, at) for piece in pieces for at in range(piece.shape[0])]
    part = held // fold
    lines = jnp.concatenate(
        [piece[at, turn * part : (turn + 1) * part, :] for turn in range(fold) for piece, at in slices],
        axis=0,
    )
    metas = jnp.concatenate([piece[at, held : held + part, :] for piece, at in slices], axis=0)
    count = lines.shape[0]
    f_at, f_lane = iota((FIELDS, LANES), 0), iota((FIELDS, LANES), 1)
    spreads = [(f_lane == f_at + turn * (LANES // 2)).astype(f32).astype(bf16) for turn in range(fold)]
    fields = jnp.concatenate([nt_dot(spread, metas) for spread in spreads], axis=1)
    kern = lax.axis_index("kern")
    low = ((lax.axis_index("sub") * kern_count + kern) * rows).astype(f32)
    row_at = fields[3:4]
    live = (fields[6:7] > 0.5) & (row_at < low + rows) & (row_at + support > low)
    live = live.astype(f32)
    upper = (iota((count, count), 0) < iota((count, count), 1)).astype(f32).astype(bf16)
    rank = nn_dot(jnp.broadcast_to(live, (FIELDS, count)).astype(bf16), upper)[0:1]
    start = (low + rows - row_at) * live
    field_at = iota((FIELDS, count), 0)
    packed = jnp.where(field_at == 3, start, fields) * live
    pick = (iota((count, count), 0).astype(f32) == rank).astype(f32) * live
    pick = pick.astype(bf16)
    line_ref[pl.ds(0, count), :] = nn_dot(pick, lines)
    line_ref[pl.ds(count, LANES), :] = jnp.zeros((LANES, LANES), f32)
    chosen = nt_dot(packed.astype(bf16), pick)
    number = jnp.sum(live)
    screen = chosen[0:1].astype(i32)
    sizes = [screen_ref.shape[0] // (2 * support), row_tables.shape[0], OVERS]
    bits = [(size - 1).bit_length() for size in sizes]
    shifts = [sum(bits[: at + 1]) for at in range(3)]
    assert shifts[-1] + (NCOL - 1).bit_length() < 32
    me = lax.axis_index("band")
    band_of = screen // per_band
    if not direct:
        step_of = band_of
    elif band_count & (band_count - 1) == 0:
        step_of = band_of ^ me
    else:
        step_of = (band_of - me + band_count) % band_count
    within = screen % per_band
    place = step_of * share + within % share
    if splits > 1:
        place = place + ((within // share) != kern).astype(i32) * (band_count * share)
    table_row = chosen[1:2].astype(i32) * (support + 2 * rows) + chosen[3:4].astype(i32)
    col = chosen[4:5].astype(i32) * LANES + chosen[5:6].astype(i32)
    word = place
    for shift, field in zip(shifts, (table_row, chosen[2:3].astype(i32), col)):
        word = word + field * (1 << shift)
    meta_vmem[:, pl.ds(0, count)] = word
    meta_vmem[:, pl.ds(count, LANES)] = jnp.broadcast_to(number.astype(i32), (1, LANES))
    copy = pltpu.make_async_copy(meta_vmem, meta_smem, sem)
    copy.start()
    lane = iota((support, LANES), 1)
    sign = jnp.where(lane < support, -1.0, 1.0).astype(f32)
    span = NCOL // band_count

    def unfold(step, carry):
        for part_at, part in enumerate(screen_parts):
            for index in range(share):
                both = part[step, pl.ds(deep + index * support, support), :]
                turned = pltpu.roll(both.astype(f32), support, 1) * sign
                at = ((part_at * band_count + step) * share + index) * 2 * support
                at = pl.multiple_of(at, 2 * support)
                screen_ref[pl.ds(at, support), :] = both
                screen_ref[pl.ds(at + support, support), :] = turned.astype(bf16)
        total[pl.ds(pl.multiple_of(step * span, span), span), :] = jnp.zeros((span, 2 * rows), f32)
        return carry

    lax.fori_loop(0, band_count, unfold, 0)
    y_at, l_at = iota((2 * support, LANES), 0), iota((2 * support, LANES), 1)
    lag = y_at - l_at % support
    keep = ((lag >= 0) & (lag < support)).astype(f32).astype(bf16)
    wide = 2 * support
    copy.wait()

    def part_of(word, at):
        lower = shifts[at - 1] if at else 0
        high = word >> lower
        return high & ((1 << bits[at]) - 1) if at < 3 else high

    def turn(base, size, index, carry):
        ids = [base + index * size + extra for extra in range(size)]
        words = [meta_smem[0, k] for k in ids]
        for at, word in enumerate(words):
            left = row_tables[pl.ds(part_of(word, 1), rows), :].astype(bf16)
            screen_at = pl.multiple_of(part_of(word, 0) * wide, wide)
            right = screen_ref[pl.ds(screen_at, wide), :]
            half_ref[at] = nn_dot(left, right).astype(bf16)
        for at, k in enumerate(ids):
            line = jnp.broadcast_to(line_ref[pl.ds(k, 1), :], (wide, LANES))
            skew_ref[at] = pltpu.roll(line, 0, 1, stride=1, stride_axis=0).astype(bf16) * keep
        for at, word in enumerate(words):
            both = nt_dot(column_tables[part_of(word, 2)], half_ref[at]).astype(bf16)
            real, imag = both[:support], both[support:]
            kernel_ref[at, pl.ds(0, support), :] = jnp.concatenate([real, imag], axis=1)
            kernel_ref[at, pl.ds(support, support), :] = jnp.concatenate([-imag, real], axis=1)
        for at, word in enumerate(words):
            window = pl.ds(part_of(word, 3), wide)
            total[window, :] = total[window, :] + nn_dot(skew_ref[at], kernel_ref[at])
        return carry

    pieces_here = meta_smem[0, count]
    full = pieces_here // UNROLL
    left_over = pieces_here - full * UNROLL
    full = full + (left_over > LAST_TURN).astype(i32)
    lax.fori_loop(0, full, functools.partial(turn, 0, UNROLL), 0)
    short = ((left_over > 0) & (left_over <= LAST_TURN)).astype(i32)
    lax.fori_loop(0, short, functools.partial(turn, full * UNROLL, LAST_TURN), 0)
    writes = []
    for at in range(NCOL // LANES):
        turned = total[pl.ds(at * LANES, LANES), :].T
        stage[at, 0] = turned[:rows]
        stage[at, 1] = turned[rows:]
        target = out.at[:, :, pl.ds(at * LANES, LANES)]
        writes.append(pltpu.make_async_copy(stage.at[at], target, sems.at[at]))
        writes[-1].start()
    for write in writes:
        write.wait()


def table_kernel(row_source, column_source, row_tables, column_tables, sems):
    copies = [
        pltpu.make_async_copy(row_source, row_tables, sems.at[0]),
        pltpu.make_async_copy(column_source, column_tables, sems.at[1]),
    ]
    for copy in copies:
        copy.start()
    for copy in copies:
        copy.wait()


def exchange(parts, axis, count):
    if count & (count - 1) == 0:
        perms = [[(i, i ^ step) for i in range(count)] for step in range(count)]
    else:
        perms = [[((i + step) % count, i) for i in range(count)] for step in range(count)]
    return [parts[0]] + [lax.ppermute(parts[step], axis, perms[step]) for step in range(1, count)]


def program(
    screens, visibilities, vis_columns, band_route, screen_choice, offsets, row_cell, col_cell
):
    band_count = lax.axis_size("band")
    sub_count, kern_count = lax.axis_size("sub"), lax.axis_size("kern")
    per_band, _, support, _ = screens.shape
    blocks = visibilities.shape[0]
    capacity = 2 * blocks // band_count
    rows = BR // (sub_count * kern_count)
    members = sub_count * kern_count
    group = ("sub", "kern")
    direct = band_count <= DIRECT_MOST and members in (1, 2, 4)
    splits = 2 if kern_count == 2 and per_band % 2 == 0 else 1
    share = per_band // splits
    fold = 2 if direct and capacity % 16 == 0 else 1
    top = capacity + capacity // fold
    depth = top + share * support
    vmem = pl.BlockSpec(memory_space=pltpu.VMEM)
    hbm = pl.BlockSpec(memory_space=pltpu.HBM)
    grant = pltpu.CompilerParams(vmem_limit_bytes=VMEM_GRANT)
    if direct:
        messages = [jax.ShapeDtypeStruct((depth, LANES), bf16)] * band_count
    else:
        messages = [jax.ShapeDtypeStruct((band_count, depth, LANES), bf16)]
    sent = pl.pallas_call(
        functools.partial(send_kernel, band_count, splits, capacity, fold, direct),
        out_shape=messages,
        in_specs=[hbm] * 8,
        out_specs=[vmem] * len(messages),
        scratch_shapes=[
            pltpu.VMEM((share,) + screens.shape[1:], bf16),
            pltpu.VMEM(visibilities.shape, bf16),
            pltpu.VMEM(vis_columns.shape, i32),
            pltpu.VMEM((1, blocks), i32),
            pltpu.VMEM((1, blocks), i32),
            pltpu.VMEM((2, blocks), i32),
            pltpu.VMEM((1, blocks), i32),
            pltpu.VMEM((1, blocks), i32),
            pltpu.VMEM((2, blocks, support), f32),
            pltpu.VMEM((band_count * capacity, 2 * LANES), f32),
            pltpu.SemaphoreType.DMA((8,)),
        ],
        compiler_params=grant,
    )(
        *map(
            in_hbm,
            (
                screens, visibilities, vis_columns, band_route.reshape(1, blocks),
                screen_choice.reshape(1, blocks), offsets.T, row_cell.reshape(1, blocks),
                col_cell.reshape(1, blocks),
            ),
        )
    )
    count = members * band_count * capacity
    if direct:
        own = jnp.stack(exchange(sent, "band", band_count))
        slots = own[:, :top]
        pieces, screen_parts, held, deep = [own], [own], capacity, top
        for step in range(1, members):
            whole = splits > 1 and step == 1
            perm = [(i, i ^ step) for i in range(members)]
            got = lax.ppermute(own if whole else slots, group, perm)
            pieces.append(got)
            if whole:
                screen_parts.append(got)
    else:
        own = lax.all_to_all(sent[0], "band", 0, 0, tiled=True)
        slots = lax.all_gather(own[:, : 2 * capacity], group, axis=0, tiled=True)
        slots = slots.reshape(members * band_count, 2, capacity, LANES)
        pieces = [slots.transpose(1, 0, 2, 3).reshape(1, 2 * count, LANES)]
        screen_parts, held, deep = [own[:, 2 * capacity :]], count, 0
        if splits > 1:
            perm = [(i, i ^ 1) for i in range(kern_count)]
            screen_parts.append(lax.ppermute(screen_parts[0], "kern", perm))
    tables = [jnp.asarray(table) for table in table_constants(support, rows)]
    tables = pl.pallas_call(
        table_kernel,
        out_shape=[jax.ShapeDtypeStruct(table.shape, table.dtype) for table in tables],
        in_specs=[hbm] * 2,
        out_specs=[vmem] * 2,
        scratch_shapes=[pltpu.SemaphoreType.DMA((2,))],
        compiler_params=grant,
        cost_estimate=pl.CostEstimate(flops=0, bytes_accessed=1 << 21, transcendentals=0),
    )(*map(in_hbm, tables))
    parts_of = (len(pieces), len(pieces) + len(screen_parts))
    return pl.pallas_call(
        functools.partial(
            grid_kernel, band_count, kern_count, splits, held, fold, deep, per_band, rows, support,
            direct, parts_of,
        ),
        out_shape=jax.ShapeDtypeStruct((2, rows, NCOL), f32),
        in_specs=[vmem] * (parts_of[1] + 2),
        out_specs=hbm,
        scratch_shapes=[
            pltpu.VMEM((per_band * band_count * 2 * support, LANES), bf16),
            pltpu.VMEM((count + LANES, LANES), f32),
            pltpu.VMEM((1, count + LANES), i32),
            pltpu.SMEM((1, count + LANES), i32),
            pltpu.VMEM((NCOL, 2 * rows), f32),
            pltpu.VMEM((UNROLL, rows, 2 * support), bf16),
            pltpu.VMEM((UNROLL, 2 * support, 2 * rows), bf16),
            pltpu.VMEM((UNROLL, 2 * support, 2 * support), bf16),
            pltpu.VMEM((NCOL // LANES, 2, rows, LANES), f32),
            pltpu.SemaphoreType.DMA(()),
            pltpu.SemaphoreType.DMA((NCOL // LANES,)),
        ],
        compiler_params=grant,
    )(*pieces, *screen_parts, *tables)


def solution(mesh):
    in_specs = (
        P("band", None, None, None),
        P(("grp", "band", "sub", "kern"), None, None),
        P(("grp", "band", "sub", "kern"), None),
        P(("grp", "band", "sub", "kern"), None),
        P(("grp", "band", "sub", "kern")),
        P(("grp", "band", "sub", "kern"), None),
        P(("grp", "band", "sub", "kern")),
        P(("grp", "band", "sub", "kern")),
    )
    out_specs = P(None, ("grp", "band", "sub", "kern"), None)
    return jax.shard_map(program, mesh=mesh, in_specs=in_specs, out_specs=out_specs, check_vma=False)
```

```python
import functools
import math

import jax
import jax.numpy as jnp
import numpy as np
from jax import lax
from jax.experimental import pallas as pl
from jax.experimental.pallas import tpu as pltpu
from jax.sharding import PartitionSpec as P


OVERS = 8
BR = 256
NCOL = 1024
LANES = 128
FIELDS = 8
UNROLL = 60
LAST_TURN = 48
DIRECT_MOST = 4
VMEM_GRANT = 24 * 1024 * 1024

f32, bf16, i32 = jnp.float32, jnp.bfloat16, jnp.int32


def dft_tables(support):
    centred = np.arange(support, dtype=np.float32) - np.float32(support // 2)
    fractions = np.arange(OVERS, dtype=np.float32) / np.float32(OVERS)
    frequency = centred[None, :, None] + fractions[:, None, None]
    phases = np.float32(-2.0 * math.pi) * frequency * centred[None, None, :] / np.float32(support)
    scale = np.float32(support)
    return (
        (np.cos(phases) / scale).astype(jnp.bfloat16).astype(np.float32),
        (np.sin(phases) / scale).astype(jnp.bfloat16).astype(np.float32),
    )


def table_constants(support, rows):
    real, imag = dft_tables(support)
    padded = np.zeros((OVERS, support + 2 * rows, 2 * support), np.float32)
    padded[:, rows : rows + support] = np.concatenate([real, imag], axis=2)
    top = np.concatenate([real, -imag], axis=2)
    low = np.concatenate([imag, real], axis=2)
    columns = np.concatenate([top, low], axis=1).astype(jnp.bfloat16)
    return padded.reshape(-1, 2 * support), columns


def in_hbm(array):
    return pltpu.with_memory_space_constraint(array, pltpu.HBM)


def iota(shape, axis):
    return lax.broadcasted_iota(i32, shape, axis)


def nt_dot(left, right):
    return lax.dot_general(left, right, (((1,), (1,)), ((), ())), preferred_element_type=f32)


def nn_dot(left, right):
    return jnp.dot(left, right, preferred_element_type=f32)


def send_kernel(
    band_count, splits, capacity, fold, direct,
    *refs,
):
    sources, outs, held = refs[:8], refs[8:-11], refs[-11:-3]
    line_ref, slot_ref, sems = refs[-3:]
    share, _, support, _ = held[0].shape
    first = lax.axis_index("kern") * share if splits > 1 else 0
    copies = []
    for index in (3, 4, 5, 6, 7, 2, 1, 0):
        source = sources[index].at[pl.ds(first, share)] if index == 0 else sources[index]
        copies.append(pltpu.make_async_copy(source, held[index], sems.at[index]))
    for copy in copies:
        copy.start()
    screens, values, columns, route, choice, offsets, row_cell, col_cell = held
    blocks, width = columns.shape
    me = lax.axis_index("band")
    for copy in copies[:5]:
        copy.wait()
    target = route[...]
    slots = band_count * capacity
    match = (iota((band_count, blocks), 0) == target).astype(f32)
    earlier = (iota((blocks, blocks), 0) < iota((blocks, blocks), 1)).astype(f32).astype(bf16)
    before = nn_dot(match.astype(bf16), earlier)
    rank = jnp.sum(before * match, axis=0, keepdims=True).astype(i32)
    slot = target * capacity + rank
    pick = (iota((slots, blocks), 0) == slot).astype(f32).astype(bf16)
    column = col_cell[...]
    fields = [
        choice[...], offsets[pl.ds(0, 1), :], offsets[pl.ds(1, 1), :], row_cell[...],
        column // LANES, column % LANES, jnp.ones_like(column), jnp.zeros_like(column),
    ]
    field_at = iota((FIELDS, blocks), 0)
    table = jnp.zeros((FIELDS, blocks), i32)
    for index, field in enumerate(fields):
        table = jnp.where(field_at == index, field, table)
    spread = (iota((FIELDS, LANES), 0) == iota((FIELDS, LANES), 1)).astype(f32).astype(bf16)
    meta = nt_dot(pick, table.astype(f32).astype(bf16)).astype(bf16)
    for copy in copies[5:]:
        copy.wait()
    none = jnp.zeros((2, width), f32)
    for block in range(0, blocks, 2):
        hits = [
            (iota((support, width), 0) == columns[pl.ds(at, 1), :]).astype(f32).astype(bf16)
            for at in (block, block + 1)
        ]
        ahead, after = values[block].astype(f32), values[block + 1].astype(f32)
        both = jnp.concatenate(
            [jnp.concatenate([ahead, none], axis=1), jnp.concatenate([none, after], axis=1)], axis=0
        )
        line = nt_dot(both.astype(bf16), jnp.concatenate(hits, axis=1))
        for at in range(4):
            line_ref[at % 2, pl.ds(block + at // 2, 1), :] = line[at : at + 1]
    at_row, at_lane = iota((support, LANES), 0), iota((support, LANES), 1)
    place_re = (at_lane == (LANES - at_row) % LANES).astype(f32).astype(bf16)
    place_im = (at_lane == support - at_row).astype(f32).astype(bf16)
    lines = nn_dot(line_ref[0].astype(bf16), place_re) + nn_dot(line_ref[1].astype(bf16), place_im)
    payload = jnp.concatenate(
        [nn_dot(pick, lines.astype(bf16)), nn_dot(meta, spread)], axis=1
    )
    slot_ref[...] = payload
    outs = outs if direct else [outs[0].at[step] for step in range(band_count)]
    for step, out in enumerate(outs):
        dest = partner(me, step, band_count) if direct else step
        mine = slot_ref[pl.ds(dest * capacity, capacity), :]
        out[pl.ds(0, capacity), :] = mine[:, :LANES].astype(bf16)
        part = capacity // fold
        metas = mine[:part, LANES:]
        if fold > 1:
            metas = metas + pltpu.roll(mine[part:, LANES:], LANES // 2, 1)
        out[pl.ds(capacity, part), :] = metas.astype(bf16)
    for index in range(share):
        both = jnp.concatenate(
            [screens[index, 0].astype(f32), screens[index, 1].astype(f32)], axis=1
        ).astype(bf16)
        for out in outs:
            out[pl.ds(capacity + capacity // fold + index * support, support), :] = both


def partner(me, step, count):
    if count & (count - 1) == 0:
        return me ^ step
    return lax.rem(me + step, count)


def grid_kernel(
    band_count, kern_count, splits, held, fold, deep, per_band, rows, support, direct, parts_of, *refs
):
    pieces, screen_parts = refs[: parts_of[0]], refs[parts_of[0] : parts_of[1]]
    row_tables, column_tables, out = refs[parts_of[1] : parts_of[1] + 3]
    screen_ref, line_ref, meta_vmem, meta_smem, total, half_ref, kernel_ref, skew_ref, stage, sem, sems = (
        refs[parts_of[1] + 3 :]
    )
    share = per_band // splits
    slices = [(piece, at) for piece in pieces for at in range(piece.shape[0])]
    part = held // fold
    lines = jnp.concatenate(
        [piece[at, turn * part : (turn + 1) * part, :] for turn in range(fold) for piece, at in slices],
        axis=0,
    )
    metas = jnp.concatenate([piece[at, held : held + part, :] for piece, at in slices], axis=0)
    count = lines.shape[0]
    f_at, f_lane = iota((FIELDS, LANES), 0), iota((FIELDS, LANES), 1)
    spreads = [(f_lane == f_at + turn * (LANES // 2)).astype(f32).astype(bf16) for turn in range(fold)]
    fields = jnp.concatenate([nt_dot(spread, metas) for spread in spreads], axis=1)
    kern = lax.axis_index("kern")
    low = ((lax.axis_index("sub") * kern_count + kern) * rows).astype(f32)
    row_at = fields[3:4]
    live = (fields[6:7] > 0.5) & (row_at < low + rows) & (row_at + support > low)
    live = live.astype(f32)
    upper = (iota((count, count), 0) < iota((count, count), 1)).astype(f32).astype(bf16)
    rank = nn_dot(jnp.broadcast_to(live, (FIELDS, count)).astype(bf16), upper)[0:1]
    start = (low + rows - row_at) * live
    field_at = iota((FIELDS, count), 0)
    packed = jnp.where(field_at == 3, start, fields) * live
    pick = (iota((count, count), 0).astype(f32) == rank).astype(f32) * live
    pick = pick.astype(bf16)
    line_ref[pl.ds(0, count), :] = nn_dot(pick, lines)
    line_ref[pl.ds(count, LANES), :] = jnp.zeros((LANES, LANES), f32)
    chosen = nt_dot(packed.astype(bf16), pick)
    number = jnp.sum(live)
    screen = chosen[0:1].astype(i32)
    sizes = [screen_ref.shape[0] // (2 * support), row_tables.shape[0], OVERS]
    bits = [(size - 1).bit_length() for size in sizes]
    shifts = [sum(bits[: at + 1]) for at in range(3)]
    assert shifts[-1] + (NCOL - 1).bit_length() < 32
    me = lax.axis_index("band")
    band_of = screen // per_band
    if not direct:
        step_of = band_of
    elif band_count & (band_count - 1) == 0:
        step_of = band_of ^ me
    else:
        step_of = (band_of - me + band_count) % band_count
    within = screen % per_band
    place = step_of * share + within % share
    if splits > 1:
        place = place + ((within // share) != kern).astype(i32) * (band_count * share)
    table_row = chosen[1:2].astype(i32) * (support + 2 * rows) + chosen[3:4].astype(i32)
    col = chosen[4:5].astype(i32) * LANES + chosen[5:6].astype(i32)
    word = place
    for shift, field in zip(shifts, (table_row, chosen[2:3].astype(i32), col)):
        word = word + field * (1 << shift)
    meta_vmem[:, pl.ds(0, count)] = word
    meta_vmem[:, pl.ds(count, LANES)] = jnp.broadcast_to(number.astype(i32), (1, LANES))
    copy = pltpu.make_async_copy(meta_vmem, meta_smem, sem)
    copy.start()
    lane = iota((support, LANES), 1)
    sign = jnp.where(lane < support, -1.0, 1.0).astype(f32)
    span = NCOL // band_count

    def unfold(step, carry):
        for part_at, part in enumerate(screen_parts):
            for index in range(share):
                both = part[step, pl.ds(deep + index * support, support), :]
                turned = pltpu.roll(both.astype(f32), support, 1) * sign
                at = ((part_at * band_count + step) * share + index) * 2 * support
                at = pl.multiple_of(at, 2 * support)
                screen_ref[pl.ds(at, support), :] = both
                screen_ref[pl.ds(at + support, support), :] = turned.astype(bf16)
        total[pl.ds(pl.multiple_of(step * span, span), span), :] = jnp.zeros((span, 2 * rows), f32)
        return carry

    lax.fori_loop(0, band_count, unfold, 0)
    y_at, l_at = iota((2 * support, LANES), 0), iota((2 * support, LANES), 1)
    lag = y_at - l_at % support
    keep = ((lag >= 0) & (lag < support)).astype(f32).astype(bf16)
    wide = 2 * support
    copy.wait()

    def part_of(word, at):
        lower = shifts[at - 1] if at else 0
        high = word >> lower
        return high & ((1 << bits[at]) - 1) if at < 3 else high

    def turn(base, size, index, carry):
        ids = [base + index * size + extra for extra in range(size)]
        words = [meta_smem[0, k] for k in ids]
        for at, word in enumerate(words):
            left = row_tables[pl.ds(part_of(word, 1), rows), :].astype(bf16)
            screen_at = pl.multiple_of(part_of(word, 0) * wide, wide)
            right = screen_ref[pl.ds(screen_at, wide), :]
            half_ref[at] = nn_dot(left, right).astype(bf16)
        for at, k in enumerate(ids):
            line = jnp.broadcast_to(line_ref[pl.ds(k, 1), :], (wide, LANES))
            skew_ref[at] = pltpu.roll(line, 0, 1, stride=1, stride_axis=0).astype(bf16) * keep
        for at, word in enumerate(words):
            both = nt_dot(column_tables[part_of(word, 2)], half_ref[at]).astype(bf16)
            real, imag = both[:support], both[support:]
            kernel_ref[at, pl.ds(0, support), :] = jnp.concatenate([real, imag], axis=1)
            kernel_ref[at, pl.ds(support, support), :] = jnp.concatenate([-imag, real], axis=1)
        for at, word in enumerate(words):
            window = pl.ds(part_of(word, 3), wide)
            total[window, :] = total[window, :] + nn_dot(skew_ref[at], kernel_ref[at])
        return carry

    pieces_here = meta_smem[0, count]
    full = pieces_here // UNROLL
    left_over = pieces_here - full * UNROLL
    full = full + (left_over > LAST_TURN).astype(i32)
    lax.fori_loop(0, full, functools.partial(turn, 0, UNROLL), 0)
    short = ((left_over > 0) & (left_over <= LAST_TURN)).astype(i32)
    lax.fori_loop(0, short, functools.partial(turn, full * UNROLL, LAST_TURN), 0)
    writes = []
    for at in range(NCOL // LANES):
        turned = total[pl.ds(at * LANES, LANES), :].T
        stage[at, 0] = turned[:rows]
        stage[at, 1] = turned[rows:]
        target = out.at[:, :, pl.ds(at * LANES, LANES)]
        writes.append(pltpu.make_async_copy(stage.at[at], target, sems.at[at]))
        writes[-1].start()
    for write in writes:
        write.wait()


def table_kernel(row_source, column_source, row_tables, column_tables, sems):
    copies = [
        pltpu.make_async_copy(row_source, row_tables, sems.at[0]),
        pltpu.make_async_copy(column_source, column_tables, sems.at[1]),
    ]
    for copy in copies:
        copy.start()
    for copy in copies:
        copy.wait()


def exchange(parts, axis, count):
    if count & (count - 1) == 0:
        perms = [[(i, i ^ step) for i in range(count)] for step in range(count)]
    else:
        perms = [[((i + step) % count, i) for i in range(count)] for step in range(count)]
    return [parts[0]] + [lax.ppermute(parts[step], axis, perms[step]) for step in range(1, count)]


def program(
    screens, visibilities, vis_columns, band_route, screen_choice, offsets, row_cell, col_cell
):
    band_count = lax.axis_size("band")
    sub_count, kern_count = lax.axis_size("sub"), lax.axis_size("kern")
    per_band, _, support, _ = screens.shape
    blocks = visibilities.shape[0]
    capacity = 2 * blocks // band_count
    rows = BR // (sub_count * kern_count)
    members = sub_count * kern_count
    group = ("sub", "kern")
    direct = band_count <= DIRECT_MOST and members in (1, 2, 4)
    splits = 2 if kern_count == 2 and per_band % 2 == 0 else 1
    share = per_band // splits
    fold = 2 if direct and capacity % 16 == 0 else 1
    top = capacity + capacity // fold
    depth = top + share * support
    vmem = pl.BlockSpec(memory_space=pltpu.VMEM)
    hbm = pl.BlockSpec(memory_space=pltpu.HBM)
    grant = pltpu.CompilerParams(vmem_limit_bytes=VMEM_GRANT)
    if direct:
        messages = [jax.ShapeDtypeStruct((depth, LANES), bf16)] * band_count
    else:
        messages = [jax.ShapeDtypeStruct((band_count, depth, LANES), bf16)]
    sent = pl.pallas_call(
        functools.partial(send_kernel, band_count, splits, capacity, fold, direct),
        out_shape=messages,
        in_specs=[hbm] * 8,
        out_specs=[vmem] * len(messages),
        scratch_shapes=[
            pltpu.VMEM((share,) + screens.shape[1:], bf16),
            pltpu.VMEM(visibilities.shape, bf16),
            pltpu.VMEM(vis_columns.shape, i32),
            pltpu.VMEM((1, blocks), i32),
            pltpu.VMEM((1, blocks), i32),
            pltpu.VMEM((2, blocks), i32),
            pltpu.VMEM((1, blocks), i32),
            pltpu.VMEM((1, blocks), i32),
            pltpu.VMEM((2, blocks, support), f32),
            pltpu.VMEM((band_count * capacity, 2 * LANES), f32),
            pltpu.SemaphoreType.DMA((8,)),
        ],
        compiler_params=grant,
    )(
        *map(
            in_hbm,
            (
                screens, visibilities, vis_columns, band_route.reshape(1, blocks),
                screen_choice.reshape(1, blocks), offsets.T, row_cell.reshape(1, blocks),
                col_cell.reshape(1, blocks),
            ),
        )
    )
    count = members * band_count * capacity
    if direct:
        own = jnp.stack(exchange(sent, "band", band_count))
        slots = own[:, :top]
        pieces, screen_parts, held, deep = [own], [own], capacity, top
        for step in range(1, members):
            whole = splits > 1 and step == 1
            perm = [(i, i ^ step) for i in range(members)]
            got = lax.ppermute(own if whole else slots, group, perm)
            pieces.append(got)
            if whole:
                screen_parts.append(got)
    else:
        own = lax.all_to_all(sent[0], "band", 0, 0, tiled=True)
        slots = lax.all_gather(own[:, : 2 * capacity], group, axis=0, tiled=True)
        slots = slots.reshape(members * band_count, 2, capacity, LANES)
        pieces = [slots.transpose(1, 0, 2, 3).reshape(1, 2 * count, LANES)]
        screen_parts, held, deep = [own[:, 2 * capacity :]], count, 0
        if splits > 1:
            perm = [(i, i ^ 1) for i in range(kern_count)]
            screen_parts.append(lax.ppermute(screen_parts[0], "kern", perm))
    tables = [jnp.asarray(table) for table in table_constants(support, rows)]
    tables = pl.pallas_call(
        table_kernel,
        out_shape=[jax.ShapeDtypeStruct(table.shape, table.dtype) for table in tables],
        in_specs=[hbm] * 2,
        out_specs=[vmem] * 2,
        scratch_shapes=[pltpu.SemaphoreType.DMA((2,))],
        compiler_params=grant,
        cost_estimate=pl.CostEstimate(flops=0, bytes_accessed=1 << 21, transcendentals=0),
    )(*map(in_hbm, tables))
    parts_of = (len(pieces), len(pieces) + len(screen_parts))
    return pl.pallas_call(
        functools.partial(
            grid_kernel, band_count, kern_count, splits, held, fold, deep, per_band, rows, support,
            direct, parts_of,
        ),
        out_shape=jax.ShapeDtypeStruct((2, rows, NCOL), f32),
        in_specs=[vmem] * (parts_of[1] + 2),
        out_specs=hbm,
        scratch_shapes=[
            pltpu.VMEM((per_band * band_count * 2 * support, LANES), bf16),
            pltpu.VMEM((count + LANES, LANES), f32),
            pltpu.VMEM((1, count + LANES), i32),
            pltpu.SMEM((1, count + LANES), i32),
            pltpu.VMEM((NCOL, 2 * rows), f32),
            pltpu.VMEM((UNROLL, rows, 2 * support), bf16),
            pltpu.VMEM((UNROLL, 2 * support, 2 * rows), bf16),
            pltpu.VMEM((UNROLL, 2 * support, 2 * support), bf16),
            pltpu.VMEM((NCOL // LANES, 2, rows, LANES), f32),
            pltpu.SemaphoreType.DMA(()),
            pltpu.SemaphoreType.DMA((NCOL // LANES,)),
        ],
        compiler_params=grant,
    )(*pieces, *screen_parts, *tables)


def solution(mesh):
    in_specs = (
        P("band", None, None, None),
        P(("grp", "band", "sub", "kern"), None, None),
        P(("grp", "band", "sub", "kern"), None),
        P(("grp", "band", "sub", "kern"), None),
        P(("grp", "band", "sub", "kern")),
        P(("grp", "band", "sub", "kern"), None),
        P(("grp", "band", "sub", "kern")),
        P(("grp", "band", "sub", "kern")),
    )
    out_specs = P(None, ("grp", "band", "sub", "kern"), None)
    return jax.shard_map(program, mesh=mesh, in_specs=in_specs, out_specs=out_specs, check_vma=False)
```
